32 devices in a mesh: dp: 16 (over z, y, x), tensor: 2 (over core).
Axes of the slice: x: 2, y: 2, z: 4, core: 2. Of those that a mesh axis runs over, the one named last changes fastest.
Arguments:
- block_in: bfloat16 [13312, 1024], P('dp'), may hold values from -6 to 6
- grad_out: bfloat16 [13312, 1024], P('dp'), may hold values from -6 to 6
- query_weight: float32 [1024, 2048], P('dp', 'tensor'), may hold values from -0.1875 to 0.1875
- keyvalue_matrix: float32 [1024, 2, 1024], P('dp', None, 'tensor'), may hold values from -0.1875 to 0.1875
- output_weight: float32 [1024, 2048], P('dp', 'tensor'), may hold values from -1 to 1
- feedfwd_weight: float32 [1024, 3, 3072], P('dp', None, 'tensor'), may hold values from -0.25 to 0.25
- norm_gains: float32 [1024, 2], replicated, may hold values from 0.5 to 1.5
- head_gains: float32 [128, 2], replicated, may hold values from 0.7 to 3.2
- first_query: float32 [1024, 2048], P('dp', 'tensor'), may hold values from -0.625 to 0.625
- keyvalue_first_moment: float32 [1024, 2, 1024], P('dp', None, 'tensor'), may hold values from -0.625 to 0.625
- first_output: float32 [1024, 2048], P('dp', 'tensor'), may hold values from -0.625 to 0.625
- first_feedfwd: float32 [1024, 3, 3072], P('dp', None, 'tensor'), may hold values from -0.625 to 0.625
- first_norm: float32 [1024, 2], P('dp'), may hold values from -0.625 to 0.625
- first_head: float32 [128, 2], P('dp'), may hold values from -0.625 to 0.625
- second_query: float32 [1024, 2048], P('dp', 'tensor'), may hold values from 0.02 to 1
- keyvalue_second_moment: float32 [1024, 2, 1024], P('dp', None, 'tensor'), may hold values from 0.02 to 1
- second_output: float32 [1024, 2048], P('dp', 'tensor'), may hold values from 0.02 to 1
- second_feedfwd: float32 [1024, 3, 3072], P('dp', None, 'tensor'), may hold values from 0.02 to 1
- second_norm: float32 [1024, 2], P('dp'), may hold values from 0.02 to 1
- second_head: float32 [128, 2], P('dp'), may hold values from 0.1 to 300, as said below
Outputs:
- block_out: bfloat16 [13312, 1024], P('dp')
- grad_input: bfloat16 [13312, 1024], P('dp')
- grad_query: float32 [1024, 2048], P('dp', 'tensor')
- grad_keyvalue: float32 [1024, 2, 1024], P('dp', None, 'tensor')
- grad_output: float32 [1024, 2048], P('dp', 'tensor')
- grad_feedfwd: float32 [1024, 3, 3072], P('dp', None, 'tensor')
- grad_norm: float32 [1024, 2], P('dp')
- grad_head: float32 [128, 2], P('dp')
- new_query: float32 [1024, 2048], P('dp', 'tensor')
- new_keyvalue: float32 [1024, 2, 1024], P('dp', None, 'tensor')
- new_output: float32 [1024, 2048], P('dp', 'tensor')
- new_feedfwd: float32 [1024, 3, 3072], P('dp', None, 'tensor')
- new_norm: float32 [1024, 2], P('dp')
- new_head: float32 [128, 2], P('dp')
- new_first_query: float32 [1024, 2048], P('dp', 'tensor')
- new_first_keyvalue: float32 [1024, 2, 1024], P('dp', None, 'tensor')
- new_first_output: float32 [1024, 2048], P('dp', 'tensor')
- new_first_feedfwd: float32 [1024, 3, 3072], P('dp', None, 'tensor')
- new_first_norm: float32 [1024, 2], P('dp')
- new_first_head: float32 [128, 2], P('dp')
- new_second_query: float32 [1024, 2048], P('dp', 'tensor')
- new_second_keyvalue: float32 [1024, 2, 1024], P('dp', None, 'tensor')
- new_second_output: float32 [1024, 2048], P('dp', 'tensor')
- new_second_feedfwd: float32 [1024, 3, 3072], P('dp', None, 'tensor')
- new_second_norm: float32 [1024, 2], P('dp')
- new_second_head: float32 [128, 2], P('dp')
The draws below stay inside these ranges and needn't reach their ends.
Inputs may be any that keep to these rules, and one draw needn't show every extreme that they name: `second_head`: second moments of the head gains, positive.
All inputs are finite; a program needn't handle non-finite values.
Results may differ from the reference program's by a relative error of at most 0.039.
The reference program's roundings to bfloat16 on the way count: a program that leaves them out, or rounds other values in their place, can miss the bound.
Values may be sent and summed in bfloat16 or wider, within the bound.
No kernel may reach another device: no remote copies, remote signals or barrier semaphores. Data moves between devices by JAX's collectives and lax.ppermute only.
A program may use at most 256 MiB of HBM per device.

```python
import math
import jax
import jax.numpy as jnp
from jax import lax

MODEL_WIDTH = 1024
QUERY_HEADS = 16
KEYVALUE_HEADS = 8
HEAD_WIDTH = 128
FEEDFWD_UNITS = 3072
SEQUENCE_LENGTH = 832
SEQUENCES_LOCAL = 1
ADAM_STEP = 2
TOKENS = 13312
N_DP = 16
N_TENSOR = 2


def draw_head_gains(key, part):
    return jax.random.uniform(key, (HEAD_WIDTH, 2), jnp.float32, 0.7, 1.6)


def draw_second_head(key, part):
    low_end = 0.1
    high_end = 10.0
    level = jax.random.uniform(key, (HEAD_WIDTH, 2), jnp.float32, 0.0, 1.0)
    return jnp.exp(jnp.log(low_end) + level * (jnp.log(high_end) - jnp.log(low_end)))


def block_levels(own_key, dims, split, smallest, largest):
    def one(position, blocks):
        draws = jax.random.uniform(jax.random.fold_in(jax.random.fold_in(own_key, 6), position), (blocks,), jnp.float32, smallest / len(split), largest / len(split))
        return jnp.repeat(jnp.exp(draws), dims[position] // blocks).reshape((-1,) + (1,) * (len(dims) - position - 1))

    factor_of = one(*split[0])
    for cut in split[1:]:
        factor_of = factor_of * one(*cut)
    return factor_of


def noise(rng, extent, scale, reach, cuts=(), held_as=jnp.bfloat16):
    drawn = scale * jax.random.normal(rng, extent, jnp.float32)
    if cuts:
        drawn = drawn * block_levels(rng, extent, cuts, -0.22, 0.18)
    return jnp.clip(drawn, -reach, reach).astype(held_as)


def setup_inputs(seed: int = 0) -> dict:
    key_list = jax.random.split(jax.random.key(seed), 21)
    return {
        "block_in": noise(key_list[0], (TOKENS, MODEL_WIDTH), 1.0, 6.0, ((0, 16),)),
        "grad_out": noise(key_list[1], (TOKENS, MODEL_WIDTH), 1.0, 6.0, ((0, 16),)),
        "query_weight": noise(key_list[2], (MODEL_WIDTH, QUERY_HEADS * HEAD_WIDTH), MODEL_WIDTH ** -0.5, 0.1875, ((0, 16), (1, 2)), jnp.float32),
        "keyvalue_matrix": noise(key_list[3], (MODEL_WIDTH, 2, KEYVALUE_HEADS * HEAD_WIDTH), MODEL_WIDTH ** -0.5, 0.1875, ((0, 16), (2, 2)), jnp.float32),
        "output_weight": noise(key_list[4], (MODEL_WIDTH, QUERY_HEADS * HEAD_WIDTH), (QUERY_HEADS * HEAD_WIDTH // 64) ** -0.5, 1.0, ((0, 16), (1, 2)), jnp.float32),
        "feedfwd_weight": noise(key_list[5], (MODEL_WIDTH, 3, FEEDFWD_UNITS), (MODEL_WIDTH // 2) ** -0.5, 0.25, ((0, 16), (2, 2)), jnp.float32),
        "norm_gains": jnp.clip(1.0 + 0.1 * jax.random.normal(key_list[6], (MODEL_WIDTH, 2), jnp.float32), 0.5, 1.5),
        "head_gains": draw_head_gains(jax.random.fold_in(key_list[20], 71), 0),
        "first_query": noise(key_list[8], (MODEL_WIDTH, QUERY_HEADS * HEAD_WIDTH), 0.1, 0.625, ((0, 16), (1, 2)), jnp.float32),
        "keyvalue_first_moment": noise(key_list[9], (MODEL_WIDTH, 2, KEYVALUE_HEADS * HEAD_WIDTH), 0.1, 0.625, ((0, 16), (2, 2)), jnp.float32),
        "first_output": noise(key_list[10], (MODEL_WIDTH, QUERY_HEADS * HEAD_WIDTH), 0.1, 0.625, ((0, 16), (1, 2)), jnp.float32),
        "first_feedfwd": noise(key_list[11], (MODEL_WIDTH, 3, FEEDFWD_UNITS), 0.1, 0.625, ((0, 16), (2, 2)), jnp.float32),
        "first_norm": noise(key_list[12], (MODEL_WIDTH, 2), 0.1, 0.625, ((0, 16),), jnp.float32),
        "first_head": noise(key_list[13], (HEAD_WIDTH, 2), 0.1, 0.625, ((0, 16),), jnp.float32),
        "second_query": jnp.clip(jnp.exp(math.log(1.0) - 3.912023 * jax.random.uniform(key_list[14], (MODEL_WIDTH, QUERY_HEADS * HEAD_WIDTH), jnp.float32) ** block_levels(key_list[14], (MODEL_WIDTH, QUERY_HEADS * HEAD_WIDTH), ((0, 16), (1, 2)), -0.2, 0.2)), 0.02, 1.0),
        "keyvalue_second_moment": jnp.clip(jnp.exp(math.log(1.0) - 3.912023 * jax.random.uniform(key_list[15], (MODEL_WIDTH, 2, KEYVALUE_HEADS * HEAD_WIDTH), jnp.float32) ** block_levels(key_list[15], (MODEL_WIDTH, 2, KEYVALUE_HEADS * HEAD_WIDTH), ((0, 16), (2, 2)), -0.2, 0.2)), 0.02, 1.0),
        "second_output": jnp.clip(jnp.exp(math.log(1.0) - 3.912023 * jax.random.uniform(key_list[16], (MODEL_WIDTH, QUERY_HEADS * HEAD_WIDTH), jnp.float32) ** block_levels(key_list[16], (MODEL_WIDTH, QUERY_HEADS * HEAD_WIDTH), ((0, 16), (1, 2)), -0.2, 0.2)), 0.02, 1.0),
        "second_feedfwd": jnp.clip(jnp.exp(math.log(1.0) - 3.912023 * jax.random.uniform(key_list[17], (MODEL_WIDTH, 3, FEEDFWD_UNITS), jnp.float32) ** block_levels(key_list[17], (MODEL_WIDTH, 3, FEEDFWD_UNITS), ((0, 16), (2, 2)), -0.2, 0.2)), 0.02, 1.0),
        "second_norm": jnp.clip(jnp.exp(math.log(1.0) - 3.912023 * jax.random.uniform(key_list[18], (MODEL_WIDTH, 2), jnp.float32) ** block_levels(key_list[18], (MODEL_WIDTH, 2), ((0, 16),), -0.2, 0.2)), 0.02, 1.0),
        "second_head": draw_second_head(jax.random.fold_in(key_list[20], 71), 0),
    }


norm_eps = 1e-06
rope_base = 1000000.0

def rope_tables(length, head):
    half = head // 2
    freq = rope_base ** (-2.0 * jnp.arange(half, dtype=jnp.float32) / head)
    angle = jnp.arange(length, dtype=jnp.float32)[:, None] * freq[None, :]
    return (jnp.cos(angle), jnp.sin(angle))

def rotate(values, cosine, sine):
    half = values.shape[-1] // 2
    first = values[..., :half]
    second = values[..., half:]
    return jnp.concatenate([first * cosine - second * sine, second * cosine + first * sine], -1)

def rms_scale(values):
    return lax.rsqrt(lax.optimization_barrier(jnp.mean(values * values, -1, keepdims=True)) + norm_eps)

def norm_back(grad_normed, normed, scale):
    return scale * (grad_normed - normed * lax.optimization_barrier(jnp.mean(grad_normed * normed, -1, keepdims=True)))

def scores_of(query_vectors, key_rows):
    length = query_vectors.shape[0]
    raw = jnp.einsum('qkgd,tkd->kgqt', query_vectors.astype(jnp.float32), key_rows.astype(jnp.float32)) * HEAD_WIDTH ** (-0.5)
    causal = jnp.arange(length)[:, None] >= jnp.arange(length)[None, :]
    return jnp.where(causal, raw, -1e+30)

def attend(query_vectors, key_rows, values):
    scores = scores_of(query_vectors, key_rows)
    top = lax.optimization_barrier(jnp.max(scores, -1, keepdims=True))
    lse = top + jnp.log(lax.optimization_barrier(jnp.sum(jnp.exp(scores - top), -1, keepdims=True)))
    probs = jnp.exp(scores - lse).astype(jnp.bfloat16)
    mixed = jnp.einsum('kgqt,tkd->qkgd', probs.astype(jnp.float32), values.astype(jnp.float32))
    return (mixed.astype(jnp.bfloat16), lse)

def attend_back(query_vectors, key_rows, values, mixed, lse, mixed_gradient):
    scores = scores_of(query_vectors, key_rows)
    probs = jnp.exp(scores - lse)
    probs_half = probs.astype(jnp.bfloat16)
    grad_values = jnp.einsum('kgqt,qkgd->tkd', probs_half.astype(jnp.float32), mixed_gradient.astype(jnp.float32))
    grad_probs = jnp.einsum('qkgd,tkd->kgqt', mixed_gradient.astype(jnp.float32), values.astype(jnp.float32))
    delta = jnp.einsum('qkgd,qkgd->kgq', mixed_gradient.astype(jnp.float32), mixed.astype(jnp.float32))[..., None]
    grad_scores = (probs * (grad_probs - delta) * HEAD_WIDTH ** (-0.5)).astype(jnp.bfloat16)
    grad_query = jnp.einsum('kgqt,tkd->qkgd', grad_scores.astype(jnp.float32), key_rows.astype(jnp.float32))
    grad_keys = jnp.einsum('kgqt,qkgd->tkd', grad_scores.astype(jnp.float32), query_vectors.astype(jnp.float32))
    return (grad_query, grad_keys, grad_values)

def partials(left, right):
    rows = left.shape[0]
    width = right.shape[0]
    left_blocks = left.astype(jnp.float32).reshape(rows, N_TENSOR, -1)
    right_blocks = right.astype(jnp.float32).reshape(width, N_TENSOR, -1)
    return jnp.einsum('ltc,dtc->tld', left_blocks, right_blocks)

def block_sum(parts):
    rounded = lax.optimization_barrier(parts.astype(jnp.bfloat16))
    return lax.optimization_barrier(jnp.sum(rounded.astype(jnp.float32), 0))

def layer_pass(block_in, grad_out, query_half, keyvalue_half, output_half, feedfwd_half, norm_gains, head_gains, cosine, sine):
    tokens = SEQUENCES_LOCAL * SEQUENCE_LENGTH
    query_group = QUERY_HEADS // KEYVALUE_HEADS
    keyvalue_columns = KEYVALUE_HEADS * HEAD_WIDTH
    inputs = block_in.astype(jnp.float32)
    scale_one = rms_scale(inputs)
    normed_one = inputs * scale_one
    hidden_one = (normed_one * norm_gains[:, 0]).astype(jnp.bfloat16)
    query_vectors = jnp.dot(hidden_one, query_half, preferred_element_type=jnp.float32)
    keyvalue_projected = jnp.dot(hidden_one, keyvalue_half.reshape(MODEL_WIDTH, 2 * keyvalue_columns), preferred_element_type=jnp.float32)
    query_vectors = query_vectors.reshape(SEQUENCES_LOCAL, SEQUENCE_LENGTH, KEYVALUE_HEADS, query_group, HEAD_WIDTH)
    key_rows = keyvalue_projected[:, :keyvalue_columns].reshape(SEQUENCES_LOCAL, SEQUENCE_LENGTH, KEYVALUE_HEADS, HEAD_WIDTH)
    value_halves = keyvalue_projected[:, keyvalue_columns:].reshape(SEQUENCES_LOCAL, SEQUENCE_LENGTH, KEYVALUE_HEADS, HEAD_WIDTH).astype(jnp.bfloat16)
    query_scale = rms_scale(query_vectors)
    normalized_query = query_vectors * query_scale
    keys_scale = rms_scale(key_rows)
    normalized_keys = key_rows * keys_scale
    cos_query = cosine[None, :, None, None, :]
    sin_query = sine[None, :, None, None, :]
    cos_keys = cosine[None, :, None, :]
    sin_keys = sine[None, :, None, :]
    query_half_rot = rotate(normalized_query * head_gains[:, 0], cos_query, sin_query).astype(jnp.bfloat16)
    keys_half_rot = rotate(normalized_keys * head_gains[:, 1], cos_keys, sin_keys).astype(jnp.bfloat16)
    mixed, lse = lax.map(lambda item: attend(item[0], item[1], item[2]), (query_half_rot, keys_half_rot, value_halves))
    mixed_flat = mixed.reshape(tokens, QUERY_HEADS * HEAD_WIDTH)
    attn = block_sum(partials(mixed_flat, output_half))
    resid = inputs + attn
    scale_two = rms_scale(resid)
    normed_two = resid * scale_two
    hidden_two = (normed_two * norm_gains[:, 1]).astype(jnp.bfloat16)
    gate_up = jnp.dot(hidden_two, feedfwd_half[:, :2].reshape(MODEL_WIDTH, 2 * FEEDFWD_UNITS), preferred_element_type=jnp.float32)
    gate = gate_up[:, :FEEDFWD_UNITS]
    upper = gate_up[:, FEEDFWD_UNITS:]
    sigma = jax.nn.sigmoid(gate)
    act = (gate * sigma * upper).astype(jnp.bfloat16)
    ffn_out = block_sum(partials(act, feedfwd_half[:, 2]))
    block_out = (resid + ffn_out).astype(jnp.bfloat16)
    grad_f = grad_out.astype(jnp.float32)
    grad_act = jnp.dot(grad_out, feedfwd_half[:, 2], preferred_element_type=jnp.float32)
    grad_gate = (grad_act * upper * sigma * (1.0 + gate * (1.0 - sigma))).astype(jnp.bfloat16)
    grad_up = (grad_act * gate * sigma).astype(jnp.bfloat16)
    grad_feedfwd = jnp.stack([jnp.dot(hidden_two.T, grad_gate, preferred_element_type=jnp.float32), jnp.dot(hidden_two.T, grad_up, preferred_element_type=jnp.float32), jnp.dot(grad_out.T, act, preferred_element_type=jnp.float32)], 1)
    grad_hidden_two = block_sum(partials(grad_gate, feedfwd_half[:, 0]) + partials(grad_up, feedfwd_half[:, 1]))
    gain_two = lax.optimization_barrier(jnp.sum(grad_hidden_two * normed_two, 0))
    grad_resid = grad_f + norm_back(grad_hidden_two * norm_gains[:, 1], normed_two, scale_two)
    grad_resid_half = grad_resid.astype(jnp.bfloat16)
    grad_output = jnp.dot(grad_resid_half.T, mixed_flat, preferred_element_type=jnp.float32)
    mixed_gradient = jnp.dot(grad_resid_half, output_half, preferred_element_type=jnp.float32).astype(jnp.bfloat16)
    mixed_gradient = mixed_gradient.reshape(SEQUENCES_LOCAL, SEQUENCE_LENGTH, KEYVALUE_HEADS, query_group, HEAD_WIDTH)
    grad_q, grad_k, grad_v = lax.map(lambda item: attend_back(*item), (query_half_rot, keys_half_rot, value_halves, mixed, lse, mixed_gradient))
    query_norm_gradient = rotate(grad_q, cos_query, -sin_query)
    key_norm_gradient = rotate(grad_k, cos_keys, -sin_keys)
    per_head_query = lax.optimization_barrier(jnp.sum((query_norm_gradient * normalized_query).reshape(SEQUENCES_LOCAL, SEQUENCE_LENGTH, N_TENSOR, KEYVALUE_HEADS // N_TENSOR, query_group, HEAD_WIDTH), (0, 1, 3, 4)))
    per_head_keys = lax.optimization_barrier(jnp.sum((key_norm_gradient * normalized_keys).reshape(SEQUENCES_LOCAL, SEQUENCE_LENGTH, N_TENSOR, KEYVALUE_HEADS // N_TENSOR, HEAD_WIDTH), (0, 1, 3)))
    grad_head = block_sum(jnp.stack([per_head_query, per_head_keys], -1))
    grad_q_raw = norm_back(query_norm_gradient * head_gains[:, 0], normalized_query, query_scale).astype(jnp.bfloat16).reshape(tokens, QUERY_HEADS * HEAD_WIDTH)
    grad_k_raw = norm_back(key_norm_gradient * head_gains[:, 1], normalized_keys, keys_scale).astype(jnp.bfloat16).reshape(tokens, keyvalue_columns)
    grad_v_half = grad_v.astype(jnp.bfloat16).reshape(tokens, keyvalue_columns)
    grad_query = jnp.dot(hidden_one.T, grad_q_raw, preferred_element_type=jnp.float32)
    grad_kv_cat = jnp.concatenate([grad_k_raw, grad_v_half], 1)
    grad_keyvalue = jnp.dot(hidden_one.T, grad_kv_cat, preferred_element_type=jnp.float32).reshape(MODEL_WIDTH, 2, keyvalue_columns)
    grad_hidden_one = block_sum(partials(grad_q_raw, query_half) + partials(grad_k_raw, keyvalue_half[:, 0]) + partials(grad_v_half, keyvalue_half[:, 1]))
    gain_one = lax.optimization_barrier(jnp.sum(grad_hidden_one * normed_one, 0))
    grad_input = (grad_resid + norm_back(grad_hidden_one * norm_gains[:, 0], normed_one, scale_one)).astype(jnp.bfloat16)
    grad_norm = jnp.stack([gain_one, gain_two], 1)
    return ((block_out, grad_input), (grad_query, grad_keyvalue, grad_output, grad_feedfwd, grad_norm, grad_head))

def adam(param, grad, first, second, rate, decay):
    new_first = 0.9 * first + 0.1 * grad
    new_second = 0.95 * second + 0.05 * grad * grad
    fix_first = 1.0 - 0.9 ** ADAM_STEP
    fix_second = 1.0 - 0.95 ** ADAM_STEP
    step_size = new_first / fix_first / (jnp.sqrt(new_second / fix_second) + 1e-08)
    return (param - rate * (step_size + decay * param), new_first, new_second)

def reference(block_in, grad_out, query_weight, keyvalue_matrix, output_weight, feedfwd_weight, norm_gains, head_gains, first_query, keyvalue_first_moment, first_output, first_feedfwd, first_norm, first_head, second_query, keyvalue_second_moment, second_output, second_feedfwd, second_norm, second_head):
    query_half = query_weight.astype(jnp.bfloat16)
    keyvalue_half = keyvalue_matrix.astype(jnp.bfloat16)
    output_half = output_weight.astype(jnp.bfloat16)
    feedfwd_half = feedfwd_weight.astype(jnp.bfloat16)
    cosine, sine = rope_tables(SEQUENCE_LENGTH, HEAD_WIDTH)

    def device_pass(totals, pair):
        outputs, grads = layer_pass(pair[0], pair[1], query_half, keyvalue_half, output_half, feedfwd_half, norm_gains, head_gains, cosine, sine)
        return (jax.tree.map(lambda left, right: left + right, totals, grads), outputs)
    zero_filled = (jnp.zeros((MODEL_WIDTH, QUERY_HEADS * HEAD_WIDTH), jnp.float32), jnp.zeros((MODEL_WIDTH, 2, KEYVALUE_HEADS * HEAD_WIDTH), jnp.float32), jnp.zeros((MODEL_WIDTH, QUERY_HEADS * HEAD_WIDTH), jnp.float32), jnp.zeros((MODEL_WIDTH, 3, FEEDFWD_UNITS), jnp.float32), jnp.zeros((MODEL_WIDTH, 2), jnp.float32), jnp.zeros((HEAD_WIDTH, 2), jnp.float32))
    rows = SEQUENCES_LOCAL * SEQUENCE_LENGTH
    totals, outputs = lax.scan(device_pass, zero_filled, (block_in.reshape(N_DP, rows, MODEL_WIDTH), grad_out.reshape(N_DP, rows, MODEL_WIDTH)))
    block_out = outputs[0].reshape(N_DP * rows, MODEL_WIDTH)
    grad_input = outputs[1].reshape(N_DP * rows, MODEL_WIDTH)
    grad_scale = float(TOKENS) ** (-0.5)
    grad_query, grad_keyvalue, grad_output, grad_feedfwd, grad_norm, grad_head = jax.tree.map(lambda total: total * grad_scale, totals)
    new_query, new_first_query, new_second_query = adam(query_weight, grad_query, first_query, second_query, 0.01, 0.1)
    new_keyvalue, new_first_keyvalue, new_second_keyvalue = adam(keyvalue_matrix, grad_keyvalue, keyvalue_first_moment, keyvalue_second_moment, 0.01, 0.1)
    new_output, new_first_output, new_second_output = adam(output_weight, grad_output, first_output, second_output, 0.01, 0.1)
    new_feedfwd, new_first_feedfwd, new_second_feedfwd = adam(feedfwd_weight, grad_feedfwd, first_feedfwd, second_feedfwd, 0.01, 0.1)
    new_norm, new_first_norm, new_second_norm = adam(norm_gains, grad_norm, first_norm, second_norm, 0.1, 0.0)
    new_head, new_first_head, new_second_head = adam(head_gains, grad_head, first_head, second_head, 0.1, 0.0)
    return (block_out, grad_input, grad_query, grad_keyvalue, grad_output, grad_feedfwd, grad_norm, grad_head, new_query, new_keyvalue, new_output, new_feedfwd, new_norm, new_head, new_first_query, new_first_keyvalue, new_first_output, new_first_feedfwd, new_first_norm, new_first_head, new_second_query, new_second_keyvalue, new_second_output, new_second_feedfwd, new_second_norm, new_second_head)
```

```python
import functools

import jax
import jax.numpy as jnp
from jax import lax
from jax.experimental import pallas as pl
from jax.experimental.pallas import tpu as pltpu
from jax.sharding import PartitionSpec as P

QUERY_HEADS = 16
KEYVALUE_HEADS = 8
SEQUENCE_LENGTH = 832
ADAM_STEP = 2


norm_eps = 1e-06
rope_base = 1000000.0


def rope_tables(length, head):
    half = head // 2
    freq = rope_base ** (-2.0 * jnp.arange(half, dtype=jnp.float32) / head)
    angle = jnp.arange(length, dtype=jnp.float32)[:, None] * freq[None, :]
    return (jnp.cos(angle), jnp.sin(angle))


def rotate(values, cosine, sine):
    half = values.shape[-1] // 2
    first = values[..., :half]
    second = values[..., half:]
    return jnp.concatenate([first * cosine - second * sine, second * cosine + first * sine], -1)


def rms_scale(values):
    return lax.rsqrt(jnp.mean(values * values, -1, keepdims=True) + norm_eps)


def norm_back(grad_normed, normed, scale):
    return scale * (grad_normed - normed * jnp.mean(grad_normed * normed, -1, keepdims=True))


def dense(left, right):
    return jnp.dot(left, right, preferred_element_type=jnp.float32)


def contract_cols(left, right):
    return lax.dot_general(
        left, right, (((1,), (1,)), ((), ())), preferred_element_type=jnp.float32
    )


def contract_rows(left, right):
    return lax.dot_general(
        left, right, (((0,), (0,)), ((), ())), preferred_element_type=jnp.float32
    )


def rot_table(tokens, head):
    cosine, sine = rope_tables(tokens, head)
    return jnp.concatenate([cosine, cosine], 1), jnp.concatenate([-sine, sine], 1)


def peer_exchange(values):
    return lax.ppermute(values, "tensor", [(0, 1), (1, 0)])


def tensor_sum(partial):
    if lax.axis_size("tensor") == 2:
        return partial.astype(jnp.float32) + peer_exchange(partial).astype(jnp.float32)
    return lax.psum(partial, "tensor").astype(jnp.float32)


PIECES = [(dx, dy, half) for dx, dy in ((0, 0), (1, 0), (0, 1), (1, 1)) for half in (0, 1)]


def hop(values, kind):
    size = lax.axis_size("dp")
    if kind == "x":
        pairs = [(i, i ^ 1) for i in range(size)]
    elif kind == "y":
        pairs = [(i, i ^ 2) for i in range(size)]
    else:
        pairs = [(i, (i + 4 * kind) % size) for i in range(size)]
    return lax.ppermute(values, "dp", pairs)


def piece_offsets(sign):
    size = lax.axis_size("dp")
    line = size // 4
    me = lax.axis_index("dp")
    place = jnp.arange(line, dtype=jnp.int32)
    along = (me // 4 + sign * place + line) % line
    rows = []
    for dx, dy, half in PIECES:
        part = along[half * (line // 2) : (half + 1) * (line // 2)]
        second = (me // 2 % 2 + dy) % 2
        first = (me % 2 + dx) % 2
        rows.append(part * 4 + second * 2 + first)
    return jnp.concatenate(rows).astype(jnp.int32)


def after(values, *gates):
    return lax.optimization_barrier((values, *gates))[0]


def line_gather(values):
    line = lax.axis_size("dp") // 4
    return [values] + [hop(values, step) for step in range(1, line)]


def plane_gather(parts):
    half = len(parts) // 2
    low = jnp.stack(parts[:half])
    high = jnp.stack(parts[half:])
    x_low, x_high = hop(low, "x"), hop(high, "x")
    y_low, y_high = hop(low, "y"), hop(high, "y")
    d_low, d_high = hop(x_low, "y"), hop(y_high, "x")
    return [low, high, x_low, x_high, y_low, y_high, d_low, d_high]


def add_half(left, right):
    return (left.astype(jnp.float32) + right.astype(jnp.float32)).astype(jnp.bfloat16)


def scatter_sum(pieces):
    k_low, k_high, x_low, x_high, y_low, y_high, d_low, d_high = pieces
    line = lax.axis_size("dp") // 4
    got_d_low, got_d_high = hop(d_low, "y"), hop(d_high, "x")
    got_x_high, got_y_low = hop(x_high, "x"), hop(y_low, "y")
    got_x_low = hop(add_half(x_low, got_d_low), "x")
    got_y_high = hop(add_half(y_high, got_d_high), "y")
    low = [k_low, got_x_low, got_y_low]
    high = [k_high, got_x_high, got_y_high]

    def block(step):
        side, place = (low, step) if step < line // 2 else (high, step - line // 2)
        return sum(term[place].astype(jnp.float32) for term in side)

    total = block(0)
    for step in range(1, line):
        total = total + hop(block(step).astype(jnp.bfloat16), step).astype(jnp.float32)
    return total


def all_sum_small(values):
    size = lax.axis_size("dp")
    values = values + hop(values, "x")
    values = values + hop(values, "y")
    total = values
    for step in range(1, size // 4):
        total = total + hop(values, step)
    return total


def block_copies(pieces, buffer, offsets, sems, lead):
    rows = pieces[0].shape[-2]
    copies = []
    index = 0
    for piece in pieces:
        for place in range(piece.shape[0]):
            start = pl.multiple_of(offsets[index] * rows, rows)
            source = piece.at[place] if lead is None else piece.at[place, lead]
            target = buffer if lead is None else buffer.at[lead]
            sem = sems.at[index] if lead is None else sems.at[lead, index]
            copies.append(pltpu.make_async_copy(source, target.at[pl.ds(start, rows), :], sem))
            index += 1
    return copies


def store_blocks(total, outs, offsets, lead):
    index = 0
    for out in outs:
        rows = out.shape[-2]
        for place in range(out.shape[0]):
            start = pl.multiple_of(offsets[index] * rows, rows)
            block = total[pl.ds(start, rows), :].astype(jnp.bfloat16)
            if lead:
                out[place, 0] = block
            else:
                out[place] = block
            index += 1


def spans(size, step):
    return [(start, min(start + step, size)) for start in range(0, size, step)]


def row_spans(size):
    return spans(size, 416)


def rotate_rows(values, cos_ref, sin_ref, sign):
    turned = pltpu.roll(values, values.shape[1] // 2, 1)
    return values * cos_ref + sign * turned * sin_ref


def to_row(column):
    return jnp.broadcast_to(column, (column.shape[0], 128)).T[0:1, :]


def causal_t(first_key, keys, first_query, queries):
    key = lax.broadcasted_iota(jnp.int32, (keys, queries), 0) + first_key
    query = lax.broadcasted_iota(jnp.int32, (keys, queries), 1) + first_query
    return key <= query


LOG2E = 1.4426950408889634


def attend_kernel(
    offsets, hidden, cos_ref, sin_ref, gains, *rest, kv_count, group, head, eps, rows_step
):
    pieces, (turned, raw, mixed, lse_ref, weights, sems) = rest[:8], rest[8:]
    step = pl.program_id(0)
    tokens = hidden.shape[0]
    q_cols = group * head

    @pl.when(step == 0)
    def _():
        for lead in range(kv_count):
            for copy in block_copies(pieces, weights, offsets, sems, lead):
                copy.start()

    for copy in block_copies(pieces, weights, offsets, sems, step):
        copy.wait()
    for start, end in spans(tokens, rows_step):
        projected = dense(hidden[start:end, :], weights[step])
        raw[start:end, :] = projected[:, : q_cols + head]
        for j in range(group + 1):
            part = projected[:, j * head : (j + 1) * head]
            scale = lax.rsqrt(jnp.mean(part * part, -1, keepdims=True) + eps)
            gain = gains[0:1, :] if j < group else gains[1:2, :]
            rotated = rotate_rows(
                part * scale * gain, cos_ref[start:end, :], sin_ref[start:end, :], 1.0
            )
            turned[start:end, j * head : (j + 1) * head] = rotated.astype(jnp.bfloat16)
        turned[start:end, q_cols + head :] = projected[:, q_cols + head :].astype(jnp.bfloat16)
    factor = head ** (-0.5)
    for j in range(group):
        for start, end in spans(tokens, 256):
            query = turned[start:end, j * head : (j + 1) * head]
            keys = turned[start:end, q_cols : q_cols + head]
            scores = contract_cols(query, keys)
            row = lax.broadcasted_iota(jnp.int32, scores.shape, 0)
            col = lax.broadcasted_iota(jnp.int32, scores.shape, 1)
            scores = jnp.where(row >= col, scores, -1e30)
            top = jnp.max(scores, -1, keepdims=True)
            if start:
                before = contract_cols(query, turned[:start, q_cols : q_cols + head])
                top = jnp.maximum(top, jnp.max(before, -1, keepdims=True))
            weight = jnp.exp2((scores - top) * (factor * LOG2E))
            norm = jnp.sum(weight, -1, keepdims=True)
            if start:
                weight_before = jnp.exp2((before - top) * (factor * LOG2E))
                norm = norm + jnp.sum(weight_before, -1, keepdims=True)
            inverse = 1.0 / norm
            total = dense(
                (weight * inverse).astype(jnp.bfloat16), turned[start:end, q_cols + head :]
            )
            if start:
                total = total + dense(
                    (weight_before * inverse).astype(jnp.bfloat16),
                    turned[:start, q_cols + head :],
                )
            mixed[start:end, j * head : (j + 1) * head] = total.astype(jnp.bfloat16)
            lse_ref[0, j : j + 1, start:end] = to_row(top * factor + jnp.log(norm))


def fixed(shape):
    return pl.BlockSpec(
        shape, lambda i, off: (0,) * len(shape), pipeline_mode=pl.Buffered(buffer_count=1)
    )


ANYWHERE = pl.BlockSpec(memory_space=pl.ANY)


def params(limit=None):
    return pltpu.CompilerParams(
        dimension_semantics=("arbitrary",), vmem_limit_bytes=limit or 60 * 1024 * 1024
    )


def cost(flops, bytes_moved):
    return pl.CostEstimate(flops=int(flops), bytes_accessed=int(bytes_moved), transcendentals=0)


def attend_call(offsets, hidden, cos_two, sin_two, gains_t, pieces, kv_count, group, head):
    tokens, width = hidden.shape
    cols = (group + 2) * head
    blocks = len(PIECES) * pieces[0].shape[0]
    raw_cols = (group + 1) * head
    by_step = lambda i, off: (0, i)
    return pl.pallas_call(
        functools.partial(
            attend_kernel, kv_count=kv_count, group=group, head=head, eps=norm_eps, rows_step=416
        ),
        out_shape=(
            jax.ShapeDtypeStruct((tokens, kv_count * cols), jnp.bfloat16),
            jax.ShapeDtypeStruct((tokens, kv_count * raw_cols), jnp.float32),
            jax.ShapeDtypeStruct((tokens, kv_count * group * head), jnp.bfloat16),
            jax.ShapeDtypeStruct((kv_count, 8, tokens), jnp.float32),
        ),
        grid_spec=pltpu.PrefetchScalarGridSpec(
            num_scalar_prefetch=1,
            grid=(kv_count,),
            in_specs=[
                fixed((tokens, width)),
                fixed((tokens, head)),
                fixed((tokens, head)),
                fixed((2, head)),
            ]
            + [ANYWHERE] * 8,
            out_specs=(
                pl.BlockSpec((tokens, cols), by_step),
                pl.BlockSpec((tokens, raw_cols), by_step),
                pl.BlockSpec((tokens, group * head), by_step),
                pl.BlockSpec((1, 8, tokens), lambda i, off: (i, 0, 0)),
            ),
            scratch_shapes=[
                pltpu.VMEM((kv_count, width, cols), jnp.bfloat16),
                pltpu.SemaphoreType.DMA((kv_count, blocks)),
            ],
        ),
        compiler_params=params(),
        cost_estimate=cost(
            2 * tokens * width * cols * kv_count + 3 * tokens * tokens * head * group * kv_count,
            tokens * (width * 2 + kv_count * (cols * 2 + raw_cols * 4 + group * head * 2))
            + width * cols * kv_count * 2,
        ),
        name="attend",
    )(offsets, hidden, cos_two, sin_two, gains_t, *pieces)


def project_kernel(offsets, mixed, *rest):
    pieces, (out, weights, sems) = rest[:8], rest[8:]
    copies = block_copies(pieces, weights, offsets, sems, None)
    for copy in copies:
        copy.start()
    for copy in copies:
        copy.wait()
    for start, end in row_spans(mixed.shape[0]):
        out[start:end, :] = contract_cols(mixed[start:end, :], weights[...]).astype(jnp.bfloat16)


def project_call(offsets, mixed, pieces):
    tokens, cols = mixed.shape
    width = pieces[0].shape[1] * lax.axis_size("dp")
    blocks = len(PIECES) * pieces[0].shape[0]
    return pl.pallas_call(
        project_kernel,
        out_shape=jax.ShapeDtypeStruct((tokens, width), jnp.bfloat16),
        grid_spec=pltpu.PrefetchScalarGridSpec(
            num_scalar_prefetch=1,
            grid=(1,),
            in_specs=[fixed((tokens, cols))] + [ANYWHERE] * 8,
            out_specs=fixed((tokens, width)),
            scratch_shapes=[
                pltpu.VMEM((width, cols), jnp.bfloat16),
                pltpu.SemaphoreType.DMA((blocks,)),
            ],
        ),
        compiler_params=params(),
        cost_estimate=cost(2 * tokens * width * cols, 2 * tokens * (width + cols) + 2 * width * cols),
        name="project",
    )(offsets, mixed, *pieces)


def feed_kernel(
    load_at, store_at, hidden, hidden_t, grad, grad_t, *rest, subs, size, first, last
):
    rest = list(rest)
    if first:
        outer_in = inner_in = None
    else:
        outer_in, inner_in = rest[:2]
        rest = rest[2:]
    pieces, (outer, inner), outs = rest[:8], rest[8:10], rest[10:18]
    weights, act, d_gate, d_up, total, outer_sum, inner_sum, sems = rest[18:]
    step = pl.program_id(0)
    tokens, width = hidden.shape

    @pl.when(step == 0)
    def _():
        for lead in range(subs):
            for copy in block_copies(pieces, weights, load_at, sems, lead):
                copy.start()
        outer_sum[...] = jnp.zeros_like(outer_sum) if first else outer_in[...]
        inner_sum[...] = jnp.zeros_like(inner_sum) if first else inner_in[...]

    for copy in block_copies(pieces, weights, load_at, sems, step):
        copy.wait()
    for start, end in row_spans(tokens):
        gate = dense(hidden[start:end, :], weights[step, :, :size])
        upper = dense(hidden[start:end, :], weights[step, :, size : 2 * size])
        grad_act = dense(grad[start:end, :], weights[step, :, 2 * size :])
        sigma = jax.nn.sigmoid(gate)
        silu = gate * sigma
        act[start:end, :] = (silu * upper).astype(jnp.bfloat16)
        d_gate[start:end, :] = (
            grad_act * upper * sigma * (1.0 + gate * (1.0 - sigma))
        ).astype(jnp.bfloat16)
        d_up[start:end, :] = (grad_act * silu).astype(jnp.bfloat16)
        outer_sum[start:end, :] += contract_cols(act[start:end, :], weights[step, :, 2 * size :])
        inner_sum[start:end, :] += contract_cols(
            d_gate[start:end, :], weights[step, :, :size]
        ) + contract_cols(d_up[start:end, :], weights[step, :, size : 2 * size])
    for start, end in spans(width, 512):
        total[start:end, :size] = dense(hidden_t[start:end, :], d_gate[...])
        total[start:end, size : 2 * size] = dense(hidden_t[start:end, :], d_up[...])
        total[start:end, 2 * size :] = dense(grad_t[start:end, :], act[...])
    store_blocks(total, outs, store_at, True)

    @pl.when(step == subs - 1)
    def _():
        outer[...] = outer_sum[...].astype(outer.dtype)
        inner[...] = inner_sum[...].astype(inner.dtype)


def fixed_two(shape):
    return pl.BlockSpec(
        shape, lambda i, a, b: (0,) * len(shape), pipeline_mode=pl.Buffered(buffer_count=1)
    )


def feed_call(load_at, store_at, hidden, hidden_t, grad, grad_t, sums, pieces, size, last):
    tokens, width = hidden.shape
    places, subs, rows, cols = pieces[0].shape
    blocks = len(PIECES) * places
    first = sums is None
    kind = jnp.bfloat16 if last else jnp.float32
    whole = fixed_two((tokens, width))
    turned = fixed_two((width, tokens))
    piece_spec = pl.BlockSpec((places, 1, rows, cols), lambda i, a, b: (0, i, 0, 0))
    result = pl.pallas_call(
        functools.partial(feed_kernel, subs=subs, size=size, first=first, last=last),
        out_shape=(
            jax.ShapeDtypeStruct((tokens, width), kind),
            jax.ShapeDtypeStruct((tokens, width), kind),
        )
        + (jax.ShapeDtypeStruct((places, subs, rows, cols), jnp.bfloat16),) * 8,
        grid_spec=pltpu.PrefetchScalarGridSpec(
            num_scalar_prefetch=2,
            grid=(subs,),
            in_specs=[whole, turned, whole, turned]
            + ([] if first else [whole, whole])
            + [ANYWHERE] * 8,
            out_specs=(whole, whole) + (piece_spec,) * 8,
            scratch_shapes=[
                pltpu.VMEM((subs, width, cols), jnp.bfloat16),
                pltpu.VMEM((tokens, size), jnp.bfloat16),
                pltpu.VMEM((tokens, size), jnp.bfloat16),
                pltpu.VMEM((tokens, size), jnp.bfloat16),
                pltpu.VMEM((width, cols), jnp.float32),
                pltpu.VMEM((tokens, width), jnp.float32),
                pltpu.VMEM((tokens, width), jnp.float32),
                pltpu.SemaphoreType.DMA((subs, blocks)),
            ],
        ),
        compiler_params=params(),
        cost_estimate=cost(
            18 * tokens * width * size * subs,
            tokens * width * (8 + 16) + 4 * width * cols * subs,
        ),
        name="feed",
    )(load_at, store_at, hidden, hidden_t, grad, grad_t, *(sums or ()), *pieces)
    return result[:2], list(result[2:])


def outer_kernel(load_at, store_at, grad, grad_t, mixed, *rest, block):
    pieces, mixed_grad, outs = rest[:8], rest[8], rest[9:17]
    weights, total, sems = rest[17:]
    step = pl.program_id(0)

    @pl.when(step == 0)
    def _():
        copies = block_copies(pieces, weights, load_at, sems, None)
        for copy in copies:
            copy.start()
        for copy in copies:
            copy.wait()

    for start, end in spans(grad_t.shape[0], 512):
        total[start:end, :] = dense(grad_t[start:end, :], mixed[...])
    store_blocks(total, outs, store_at, False)
    column = pl.ds(pl.multiple_of(step * block, block), block)
    for start, end in row_spans(grad.shape[0]):
        mixed_grad[start:end, :] = dense(grad[start:end, :], weights[:, column]).astype(jnp.bfloat16)


def outer_call(load_at, store_at, grad, grad_t, mixed, pieces, block):
    tokens, width = grad.shape
    cols = mixed.shape[1]
    places, rows, _ = pieces[0].shape
    blocks = len(PIECES) * places
    piece_spec = pl.BlockSpec((places, rows, block), lambda i, a, b: (0, 0, i))
    by_step = pl.BlockSpec((tokens, block), lambda i, a, b: (0, i))
    result = pl.pallas_call(
        functools.partial(outer_kernel, block=block),
        out_shape=(jax.ShapeDtypeStruct((tokens, cols), jnp.bfloat16),)
        + (jax.ShapeDtypeStruct((places, rows, cols), jnp.bfloat16),) * 8,
        grid_spec=pltpu.PrefetchScalarGridSpec(
            num_scalar_prefetch=2,
            grid=(cols // block,),
            in_specs=[fixed_two((tokens, width)), fixed_two((width, tokens)), by_step]
            + [ANYWHERE] * 8,
            out_specs=(by_step,) + (piece_spec,) * 8,
            scratch_shapes=[
                pltpu.VMEM((width, cols), jnp.bfloat16),
                pltpu.VMEM((width, block), jnp.float32),
                pltpu.SemaphoreType.DMA((blocks,)),
            ],
        ),
        compiler_params=params(),
        cost_estimate=cost(4 * tokens * width * cols, 4 * tokens * (width + cols) + 4 * width * cols),
        name="outer",
    )(load_at, store_at, grad, grad_t, mixed, *pieces)
    return result[0], list(result[1:])


def back_kernel(
    load_at,
    store_at,
    hidden_t,
    cos_ref,
    sin_ref,
    gains,
    turned,
    raw,
    mixed,
    mixed_grad,
    lse_ref,
    *rest,
    kv_first,
    kv_count,
    group,
    head,
    eps,
    first,
):
    rest = list(rest)
    if first:
        sum_in = None
    else:
        sum_in = rest[0]
        rest = rest[1:]
    pieces, hidden_sum, head_sum, outs = rest[:8], rest[8], rest[9], rest[10:18]
    weights, d_query, d_key, d_value, d_all, total, sems = rest[18:]
    step = pl.program_id(0)
    tokens = raw.shape[0]
    width = hidden_t.shape[0]
    q_cols = group * head
    factor = head ** (-0.5)

    @pl.when(step == 0)
    def _():
        for lead in range(kv_count):
            for copy in back_copies(pieces, weights, load_at, sems, kv_first, lead):
                copy.start()
        head_sum[...] = jnp.zeros_like(head_sum)
        hidden_sum[...] = jnp.zeros_like(hidden_sum) if first else sum_in[...]

    d_key[...] = jnp.zeros_like(d_key)
    d_value[...] = jnp.zeros_like(d_value)
    for j in range(group):
        cols = slice(j * head, (j + 1) * head)
        for start, end in spans(tokens, 256):
            query = turned[start:end, cols]
            grad = mixed_grad[start:end, cols]
            delta = to_row(
                jnp.sum(
                    grad.astype(jnp.float32) * mixed[start:end, cols].astype(jnp.float32),
                    -1,
                    keepdims=True,
                )
            )
            shift = lse_ref[0, j : j + 1, start:end] * LOG2E
            grad_query = None
            for low, high in ((0, start), (start, end)):
                if low == high:
                    continue
                keys = turned[low:high, q_cols : q_cols + head]
                values = turned[low:high, q_cols + head :]
                scores = contract_cols(keys, query)
                probs = jnp.exp2(scores * (factor * LOG2E) - shift)
                if low == start:
                    probs = jnp.where(causal_t(0, high - low, 0, end - start), probs, 0.0)
                grad_probs = contract_cols(values, grad)
                grad_scores = (probs * (grad_probs - delta) * factor).astype(jnp.bfloat16)
                d_value[low:high, :] += dense(probs.astype(jnp.bfloat16), grad)
                d_key[low:high, :] += dense(grad_scores, query)
                term = contract_rows(grad_scores, keys)
                grad_query = term if grad_query is None else grad_query + term
            d_query[start:end, cols] = grad_query
    sums = [None, None]
    for j in range(group + 1):
        cols = slice(j * head, (j + 1) * head)
        which = 0 if j < group else 1
        for start, end in row_spans(tokens):
            part = raw[start:end, cols]
            scale = lax.rsqrt(jnp.mean(part * part, -1, keepdims=True) + eps)
            normed = part * scale
            grad = d_query[start:end, cols] if j < group else d_key[start:end, :]
            grad = rotate_rows(grad, cos_ref[start:end, :], sin_ref[start:end, :], -1.0)
            product = jnp.sum(grad * normed, 0, keepdims=True)
            sums[which] = product if sums[which] is None else sums[which] + product
            grad = grad * gains[which : which + 1, :]
            d_all[start:end, cols] = (
                scale * (grad - normed * jnp.mean(grad * normed, -1, keepdims=True))
            ).astype(jnp.bfloat16)
    head_sum[0:1, :] += sums[0]
    head_sum[1:2, :] += sums[1]
    d_all[:, q_cols + head :] = d_value[...].astype(jnp.bfloat16)
    for start, end in spans(width, 512):
        total[start:end, :] = dense(hidden_t[start:end, :], d_all[...])
    store_blocks(total, outs, store_at, True)
    for copy in back_copies(pieces, weights, load_at, sems, kv_first, step):
        copy.wait()
    for start, end in row_spans(tokens):
        hidden_sum[start:end, :] += contract_cols(d_all[start:end, :], weights[step])


def back_copies(pieces, buffer, offsets, sems, kv_first, lead):
    rows = pieces[0].shape[-2]
    copies = []
    index = 0
    for piece in pieces:
        for place in range(piece.shape[0]):
            start = pl.multiple_of(offsets[index] * rows, rows)
            copies.append(
                pltpu.make_async_copy(
                    piece.at[place, kv_first + lead],
                    buffer.at[lead, pl.ds(start, rows), :],
                    sems.at[lead, index],
                )
            )
            index += 1
    return copies


def back_call(
    load_at, store_at, hidden_t, tables, kept, mixed_grad, sum_in, pieces, kv_first, kv_count, group, head
):
    cos_two, sin_two, gains_t = tables
    turned, raw, mixed, lse_t = kept
    width, tokens = hidden_t.shape
    cols = (group + 2) * head
    raw_cols = (group + 1) * head
    places, _, rows, _ = pieces[0].shape
    blocks = len(PIECES) * places
    first = sum_in is None
    by_step = lambda i, a, b: (0, kv_first + i)
    whole = fixed_two((tokens, width))
    result = pl.pallas_call(
        functools.partial(
            back_kernel,
            kv_first=kv_first,
            kv_count=kv_count,
            group=group,
            head=head,
            eps=norm_eps,
            first=first,
        ),
        out_shape=(
            jax.ShapeDtypeStruct((tokens, width), jnp.float32),
            jax.ShapeDtypeStruct((8, head), jnp.float32),
        )
        + (jax.ShapeDtypeStruct((places, kv_count, rows, cols), jnp.bfloat16),) * 8,
        grid_spec=pltpu.PrefetchScalarGridSpec(
            num_scalar_prefetch=2,
            grid=(kv_count,),
            in_specs=[
                fixed_two((width, tokens)),
                fixed_two((tokens, head)),
                fixed_two((tokens, head)),
                fixed_two((2, head)),
                pl.BlockSpec((tokens, cols), by_step),
                pl.BlockSpec((tokens, raw_cols), by_step),
                pl.BlockSpec((tokens, group * head), by_step),
                pl.BlockSpec((tokens, group * head), by_step),
                pl.BlockSpec((1, 8, tokens), lambda i, a, b: (kv_first + i, 0, 0)),
            ]
            + ([] if first else [whole])
            + [ANYWHERE] * 8,
            out_specs=(whole, fixed_two((8, head)))
            + (pl.BlockSpec((places, 1, rows, cols), lambda i, a, b: (0, i, 0, 0)),) * 8,
            scratch_shapes=[
                pltpu.VMEM((kv_count, width, cols), jnp.bfloat16),
                pltpu.VMEM((tokens, group * head), jnp.float32),
                pltpu.VMEM((tokens, head), jnp.float32),
                pltpu.VMEM((tokens, head), jnp.float32),
                pltpu.VMEM((tokens, cols), jnp.bfloat16),
                pltpu.VMEM((width, cols), jnp.float32),
                pltpu.SemaphoreType.DMA((kv_count, blocks)),
            ],
        ),
        compiler_params=params(),
        cost_estimate=cost(
            4 * tokens * width * cols * kv_count + 7 * tokens * tokens * head * group * kv_count,
            tokens * (width * 6 + kv_count * (cols * 2 + raw_cols * 4 + group * head * 4))
            + width * cols * kv_count * 4,
        ),
        name="back",
    )(
        load_at,
        store_at,
        hidden_t,
        cos_two,
        sin_two,
        gains_t,
        turned,
        raw,
        mixed,
        mixed_grad,
        lse_t,
        *(() if first else (sum_in,)),
        *pieces,
    )
    return result[0], result[1], list(result[2:])


def adam(param, grad, first, second, rate, decay):
    new_first = 0.9 * first + 0.1 * grad
    new_second = 0.95 * second + 0.05 * grad * grad
    fix_first = 1.0 - 0.9**ADAM_STEP
    fix_second = 1.0 - 0.95**ADAM_STEP
    step_size = new_first / fix_first / (jnp.sqrt(new_second / fix_second) + 1e-08)
    return (param - rate * (step_size + decay * param), new_first, new_second)


def own_rows(full, count):
    return lax.dynamic_slice_in_dim(full, lax.axis_index("dp") * count, count, 0)


def local(
    block_in,
    grad_out,
    query_weight,
    keyvalue_matrix,
    output_weight,
    feedfwd_weight,
    norm_gains,
    head_gains,
    first_query,
    keyvalue_first_moment,
    first_output,
    first_feedfwd,
    first_norm,
    first_head,
    second_query,
    keyvalue_second_moment,
    second_output,
    second_feedfwd,
    second_norm,
    second_head,
):
    tokens = block_in.shape[0]
    width = block_in.shape[1]
    head_size = head_gains.shape[0]
    group = QUERY_HEADS // KEYVALUE_HEADS
    keyvalue_columns = keyvalue_matrix.shape[2]
    kv_local = keyvalue_columns // head_size
    ffn_local = feedfwd_weight.shape[2]
    own = query_weight.shape[0]
    q_cols = group * head_size
    half_type = jnp.bfloat16
    grad_scale = float(tokens * lax.axis_size("dp")) ** (-0.5)
    load_at, store_at = piece_offsets(-1), piece_offsets(1)
    size = 256 if ffn_local % 512 == 0 else 128
    per_call = 2 if ffn_local % (2 * size) == 0 else 1
    if ffn_local // (per_call * size) > 3 or ffn_local % (per_call * size):
        per_call = ffn_local // size
    calls = ffn_local // (per_call * size)

    packed = jnp.stack(
        [
            jnp.concatenate(
                [
                    query_weight[:, n * q_cols : (n + 1) * q_cols],
                    keyvalue_matrix[:, 0, n * head_size : (n + 1) * head_size],
                    keyvalue_matrix[:, 1, n * head_size : (n + 1) * head_size],
                ],
                1,
            ).astype(half_type)
            for n in range(kv_local)
        ]
    )
    feed_parts = []
    for c in range(calls):
        blocks = []
        for b in range(c * per_call, (c + 1) * per_call):
            blocks.append(
                jnp.concatenate(
                    [feedfwd_weight[:, t, b * size : (b + 1) * size] for t in range(3)], 1
                ).astype(half_type)
            )
        feed_parts.append(jnp.stack(blocks))
    lines = line_gather(packed)
    qkv_pieces = plane_gather(lines)
    lines = line_gather(after(output_weight.astype(half_type), lines[-1]))
    out_pieces = plane_gather(lines)
    feed_pieces = []
    for part in feed_parts:
        lines = line_gather(after(part, lines[-1]))
        feed_pieces.append(plane_gather(lines))

    tables = rot_table(tokens, head_size) + (head_gains.T,)
    inputs = block_in.astype(jnp.float32)
    scale_one = rms_scale(inputs)
    normed_one = inputs * scale_one
    hidden_one = (normed_one * norm_gains[:, 0]).astype(half_type)
    hidden_one_t = hidden_one.T
    grad_out_t = grad_out.T
    kept = attend_call(load_at, hidden_one, *tables, qkv_pieces, kv_local, group, head_size)
    mixed = kept[2]
    attn = tensor_sum(project_call(load_at, mixed, out_pieces))
    resid = inputs + attn
    scale_two = rms_scale(resid)
    normed_two = resid * scale_two
    hidden_two = (normed_two * norm_gains[:, 1]).astype(half_type)
    hidden_two_t = hidden_two.T

    sums = None
    feed_rows = []
    for c in range(calls):
        sums, grads = feed_call(
            load_at,
            store_at,
            hidden_two,
            hidden_two_t,
            grad_out,
            grad_out_t,
            sums,
            feed_pieces[c],
            size,
            c == calls - 1,
        )
        feed_rows.append(scatter_sum(grads))
    ffn_half, grad_hidden_half = sums
    grad_hidden_two = tensor_sum(grad_hidden_half)
    block_out = (resid + tensor_sum(ffn_half)).astype(half_type)
    gain_two = jnp.sum(grad_hidden_two * normed_two, 0)
    grad_resid = grad_out.astype(jnp.float32) + norm_back(
        grad_hidden_two * norm_gains[:, 1], normed_two, scale_two
    )
    grad_resid_half = grad_resid.astype(half_type)
    mixed_gradient, grads = outer_call(
        load_at, store_at, grad_resid_half, grad_resid_half.T, mixed, out_pieces, q_cols
    )
    output_rows = scatter_sum(grads)
    hidden_part = None
    head_part = None
    packed_rows = []
    back_calls = 2 if kv_local % 2 == 0 else 1
    for c in range(back_calls):
        count = kv_local // back_calls
        hidden_part, heads, grads = back_call(
            load_at,
            store_at,
            hidden_one_t,
            tables,
            kept,
            mixed_gradient,
            hidden_part,
            qkv_pieces,
            c * count,
            count,
            group,
            head_size,
        )
        head_part = heads if head_part is None else head_part + heads
        packed_rows.append(scatter_sum(grads))
    grad_hidden_one = tensor_sum(hidden_part.astype(half_type))
    head_both = tensor_sum(head_part[:2].T.astype(half_type))
    gain_one = jnp.sum(grad_hidden_one * normed_one, 0)
    grad_input = (
        grad_resid + norm_back(grad_hidden_one * norm_gains[:, 0], normed_one, scale_one)
    ).astype(half_type)
    small = jnp.concatenate(
        [gain_one.reshape(-1, 128), gain_two.reshape(-1, 128), head_both.T.reshape(-1, 128)]
    )
    small = all_sum_small(small)
    lanes = width // 128
    grad_norm = jnp.stack(
        [small[:lanes].reshape(width), small[lanes : 2 * lanes].reshape(width)], 1
    )
    grad_head = small[2 * lanes :].reshape(2, head_size).T
    norm_rows = own_rows(grad_norm, first_norm.shape[0]) * grad_scale
    head_rows = own_rows(grad_head, first_head.shape[0]) * grad_scale

    by_head = jnp.concatenate(packed_rows)
    query_rows = jnp.concatenate([by_head[n, :, :q_cols] for n in range(kv_local)], 1) * grad_scale
    keyvalue_rows = (
        jnp.stack(
            [
                jnp.concatenate(
                    [
                        by_head[n, :, q_cols + t * head_size : q_cols + (t + 1) * head_size]
                        for n in range(kv_local)
                    ],
                    1,
                )
                for t in range(2)
            ],
            1,
        )
        * grad_scale
    )
    output_rows = output_rows * grad_scale
    by_block = jnp.concatenate(feed_rows)
    feedfwd_grad_rows = (
        jnp.stack(
            [
                jnp.concatenate(
                    [
                        by_block[b, :, t * size : (t + 1) * size]
                        for b in range(ffn_local // size)
                    ],
                    1,
                )
                for t in range(3)
            ],
            1,
        )
        * grad_scale
    )
    norm_own = own_rows(norm_gains, first_norm.shape[0])
    head_own = own_rows(head_gains, first_head.shape[0])
    new_query, new_first_query, new_second_query = adam(
        query_weight, query_rows, first_query, second_query, 0.01, 0.1
    )
    new_keyvalue, new_first_keyvalue, new_second_keyvalue = adam(
        keyvalue_matrix, keyvalue_rows, keyvalue_first_moment, keyvalue_second_moment, 0.01, 0.1
    )
    new_output, new_first_output, new_second_output = adam(
        output_weight, output_rows, first_output, second_output, 0.01, 0.1
    )
    new_feedfwd, new_first_feedfwd, new_second_feedfwd = adam(
        feedfwd_weight, feedfwd_grad_rows, first_feedfwd, second_feedfwd, 0.01, 0.1
    )
    new_norm, new_first_norm, new_second_norm = adam(
        norm_own, norm_rows, first_norm, second_norm, 0.1, 0.0
    )
    new_head, new_first_head, new_second_head = adam(
        head_own, head_rows, first_head, second_head, 0.1, 0.0
    )
    return (
        block_out,
        grad_input,
        query_rows,
        keyvalue_rows,
        output_rows,
        feedfwd_grad_rows,
        norm_rows,
        head_rows,
        new_query,
        new_keyvalue,
        new_output,
        new_feedfwd,
        new_norm,
        new_head,
        new_first_query,
        new_first_keyvalue,
        new_first_output,
        new_first_feedfwd,
        new_first_norm,
        new_first_head,
        new_second_query,
        new_second_keyvalue,
        new_second_output,
        new_second_feedfwd,
        new_second_norm,
        new_second_head,
    )


def solution(mesh):
    placed = (
        P("dp", None),
        P("dp", None),
        P("dp", "tensor"),
        P("dp", None, "tensor"),
        P("dp", "tensor"),
        P("dp", None, "tensor"),
        P(),
        P(),
        P("dp", "tensor"),
        P("dp", None, "tensor"),
        P("dp", "tensor"),
        P("dp", None, "tensor"),
        P("dp", None),
        P("dp", None),
        P("dp", "tensor"),
        P("dp", None, "tensor"),
        P("dp", "tensor"),
        P("dp", None, "tensor"),
        P("dp", None),
        P("dp", None),
    )
    return jax.shard_map(
        local,
        mesh=mesh,
        in_specs=placed,
        out_specs=(
            P("dp", None),
            P("dp", None),
            P("dp", "tensor"),
            P("dp", None, "tensor"),
            P("dp", "tensor"),
            P("dp", None, "tensor"),
            P("dp", None),
            P("dp", None),
            P("dp", "tensor"),
            P("dp", None, "tensor"),
            P("dp", "tensor"),
            P("dp", None, "tensor"),
            P("dp", None),
            P("dp", None),
            P("dp", "tensor"),
            P("dp", None, "tensor"),
            P("dp", "tensor"),
            P("dp", None, "tensor"),
            P("dp", None),
            P("dp", None),
            P("dp", "tensor"),
            P("dp", None, "tensor"),
            P("dp", "tensor"),
            P("dp", None, "tensor"),
            P("dp", None),
            P("dp", None),
        ),
        check_vma=False,
    )
```

```python
import functools

import jax
import jax.numpy as jnp
from jax import lax
from jax.experimental import pallas as pl
from jax.experimental.pallas import tpu as pltpu
from jax.sharding import PartitionSpec as P


QUERY_HEADS = 16
KEYVALUE_HEADS = 8
ADAM_STEP = 2


DP, TP = "dp", "tensor"
ROWS, FLAT, DEEP = P(DP, None), P(DP, TP), P(DP, None, TP)
FIRST, SECOND, BOTH = "first", "second", "both"
norm_eps = 1e-06
rope_base = 1000000.0


def rope_tables(length, head):
    half = head // 2
    freq = rope_base ** (-2.0 * jnp.arange(half, dtype=jnp.float32) / head)
    angle = jnp.arange(length, dtype=jnp.float32)[:, None] * freq[None, :]
    return (jnp.cos(angle), jnp.sin(angle))


def rms_scale(values):
    return lax.rsqrt(jnp.mean(values * values, -1, keepdims=True) + norm_eps)


def norm_back(grad_normed, normed, scale):
    return scale * (grad_normed - normed * jnp.mean(grad_normed * normed, -1, keepdims=True))


def dense(left, right):
    return jnp.dot(left, right, preferred_element_type=jnp.float32)


def contract_cols(left, right):
    return lax.dot_general(
        left, right, (((1,), (1,)), ((), ())), preferred_element_type=jnp.float32
    )


def contract_rows(left, right):
    return lax.dot_general(
        left, right, (((0,), (0,)), ((), ())), preferred_element_type=jnp.float32
    )


def rot_table(tokens, head):
    cosine, sine = rope_tables(tokens, head)
    return jnp.concatenate([cosine, cosine], 1), jnp.concatenate([-sine, sine], 1)


def peer_exchange(values):
    return lax.ppermute(values, TP, [(0, 1), (1, 0)])


def tensor_terms(partial):
    if lax.axis_size(TP) == 2:
        return partial, peer_exchange(partial)
    return lax.psum(partial, TP), jnp.zeros_like(partial)


def hop(values, flip):
    size = lax.axis_size(DP)
    return lax.ppermute(values, DP, [(i, i ^ flip) for i in range(size)])


def line_length():
    return lax.axis_size(DP) // 4


def block_places():
    steps = jnp.arange(line_length(), dtype=jnp.int32) * 4
    return lax.axis_index(DP) ^ jnp.concatenate([steps + flip for flip in range(4)])


def line_gather(values):
    return [values] + [hop(values, 4 * step) for step in range(1, line_length())]


def plane_gather(parts, way):
    own = jnp.stack(parts)
    first, second = hop(own, 1), hop(own, 2)
    if way == BOTH:
        cut = len(parts) // 2
        both = [hop(first[:cut], 2), hop(second[cut:], 1)]
    elif way == SECOND:
        both = [hop(first, 2)]
    else:
        both = [hop(second, 1)]
    return [own, first, second] + both


def add_half(left, right):
    return (left.astype(jnp.float32) + right.astype(jnp.float32)).astype(jnp.bfloat16)


def plane_sum(groups, way):
    own, first, second, both = groups
    cut = line_length() // 2
    if way == BOTH:
        low, high = hop(both[:cut], 2), hop(both[cut:], 1)
        first = jnp.concatenate([add_half(first[:cut], low), first[cut:]])
        second = jnp.concatenate([second[:cut], add_half(second[cut:], high)])
    elif way == SECOND:
        first = add_half(first, hop(both, 2))
    else:
        second = add_half(second, hop(both, 1))
    terms = [own, hop(first, 1), hop(second, 2)]
    return [
        sum(term[step].astype(jnp.float32) for term in terms) for step in range(line_length())
    ]


def line_sum(parts):
    arrived = [
        hop(jnp.concatenate([part[step].astype(jnp.bfloat16) for part in parts]), 4 * step)
        for step in range(1, line_length())
    ]
    results = []
    start = 0
    for part in parts:
        end = start + part[0].shape[0]
        total = part[0]
        for block in arrived:
            total = total + block[start:end].astype(jnp.float32)
        results.append(total)
        start = end
    return results


def all_sum_small(values):
    values = values + hop(values, 1)
    values = values + hop(values, 2)
    total = values
    for step in range(1, line_length()):
        total = total + hop(values, 4 * step)
    return total


def prepare_kernel(inputs, grad, gains, hidden, hidden_t, grad_t):
    values = inputs[...].astype(jnp.float32)
    normed = values * rms_scale(values)
    result = (normed * gains[0:1, :]).astype(jnp.bfloat16)
    hidden[...] = result
    hidden_t[...] = result.T
    grad_t[...] = grad[...].T


def middle_kernel(inputs, left, right, gains, resid, hidden, hidden_t):
    attn = left[...].astype(jnp.float32) + right[...].astype(jnp.float32)
    total = inputs[...].astype(jnp.float32) + attn
    resid[...] = total
    result = (total * rms_scale(total) * gains[1:2, :]).astype(jnp.bfloat16)
    hidden[...] = result
    hidden_t[...] = result.T


def gain_rows(product, gain, tokens):
    step = pl.program_id(0)
    row = lax.broadcasted_iota(jnp.int32, product.shape, 0) + step * product.shape[0]
    product = jnp.where(row < tokens, product, 0.0)

    @pl.when(step == 0)
    def _():
        gain[...] = jnp.zeros_like(gain)

    gain[0:1, :] += jnp.sum(product, 0, keepdims=True)


def late_kernel(resid, grad, left, right, gains, result, half, half_t, gain, *, tokens):
    total = resid[...]
    scale = rms_scale(total)
    normed = total * scale
    grad_hidden = left[...].astype(jnp.float32) + right[...].astype(jnp.float32)
    gain_rows(grad_hidden * normed, gain, tokens)
    grad_resid = grad[...].astype(jnp.float32) + norm_back(
        grad_hidden * gains[1:2, :], normed, scale
    )
    result[...] = grad_resid
    rounded = grad_resid.astype(jnp.bfloat16)
    half[...] = rounded
    half_t[...] = rounded.T


def final_kernel(inputs, grad_resid, left, right, gains, result, gain, *, tokens):
    values = inputs[...].astype(jnp.float32)
    scale = rms_scale(values)
    normed = values * scale
    grad_hidden = left[...].astype(jnp.float32) + right[...].astype(jnp.float32)
    gain_rows(grad_hidden * normed, gain, tokens)
    result[...] = (
        grad_resid[...] + norm_back(grad_hidden * gains[0:1, :], normed, scale)
    ).astype(jnp.bfloat16)


def row_call(kernel, ins, outs, moved):
    tokens, width = ins[0].shape
    block = 256
    specs = {
        "r": pl.BlockSpec((block, width), lambda i: (i, 0)),
        "t": pl.BlockSpec((width, block), lambda i: (0, i)),
        "g": pl.BlockSpec((2, width), lambda i: (0, 0)),
        "s": pl.BlockSpec((8, width), lambda i: (0, 0)),
    }
    shapes = {"r": (tokens, width), "t": (width, tokens), "s": (8, width)}
    return pl.pallas_call(
        kernel,
        out_shape=tuple(jax.ShapeDtypeStruct(shapes[kind], dtype) for kind, dtype in outs),
        grid=(pl.cdiv(tokens, block),),
        in_specs=[specs["g" if value.shape[0] == 2 else "r"] for value in ins],
        out_specs=tuple(specs[kind] for kind, _ in outs),
        compiler_params=params(),
        cost_estimate=cost(20 * tokens * width, moved * tokens * width),
    )(*ins)


def block_copies(pieces, buffer, offsets, sems, lead):
    rows = pieces[0].shape[-2]
    copies = []
    index = 0
    for piece in pieces:
        for place in range(piece.shape[0]):
            start = pl.multiple_of(offsets[index] * rows, rows)
            source = piece.at[place] if lead is None else piece.at[place, lead]
            target = buffer if lead is None else buffer.at[lead]
            sem = sems.at[index] if lead is None else sems.at[lead, index]
            copies.append(pltpu.make_async_copy(source, target.at[pl.ds(start, rows), :], sem))
            index += 1
    return copies


def store_blocks(total, outs, offsets, lead):
    index = 0
    for out in outs:
        rows = out.shape[-2]
        for place in range(out.shape[0]):
            start = pl.multiple_of(offsets[index] * rows, rows)
            block = total[pl.ds(start, rows), :].astype(jnp.bfloat16)
            if lead:
                out[place, 0] = block
            else:
                out[place] = block
            index += 1


def spans(size, step):
    return [(start, min(start + step, size)) for start in range(0, size, step)]


def each_rows(size, body):
    step = 416 if size % 416 == 0 else size
    for start in range(0, size, step):
        body(slice(start, start + step))


def each_head(count, head, body):
    for index in range(count):
        body(index, slice(index * head, (index + 1) * head))


def rotate_rows(values, cos_ref, sin_ref, sign):
    turned = pltpu.roll(values, values.shape[1] // 2, 1)
    return values * cos_ref + sign * turned * sin_ref


def to_row(column):
    return jnp.broadcast_to(column, (column.shape[0], 128)).T[0:1, :]


def causal_t(first_key, keys, first_query, queries):
    key = lax.broadcasted_iota(jnp.int32, (keys, queries), 0) + first_key
    query = lax.broadcasted_iota(jnp.int32, (keys, queries), 1) + first_query
    return key <= query


LOG2E = 1.4426950408889634


def attend_kernel(
    offsets, hidden, cos_ref, sin_ref, gains, *rest, inside, pieces_count, group, head, eps
):
    pieces, (turned, raw, mixed, lse_ref, weights, sems) = rest[:pieces_count], rest[-6:]
    tokens = hidden.shape[0]
    q_cols = group * head
    rows = pieces[0].shape[-2]
    copies = []
    for piece in pieces:
        for place in range(piece.shape[0]):
            index = len(copies)
            start = pl.multiple_of(offsets[index] * rows, rows)
            copies.append(
                pltpu.make_async_copy(
                    piece.at[place, inside], weights.at[pl.ds(start, rows), :], sems.at[index]
                )
            )
    for copy in copies:
        copy.start()
    for copy in copies:
        copy.wait()

    def project(rows):
        projected = dense(hidden[rows, :], weights[...])
        raw[rows, :] = projected[:, : q_cols + head]
        for j in range(group + 1):
            part = projected[:, j * head : (j + 1) * head]
            scale = lax.rsqrt(jnp.mean(part * part, -1, keepdims=True) + eps)
            gain = gains[0:1, :] if j < group else gains[1:2, :]
            rotated = rotate_rows(part * scale * gain, cos_ref[rows, :], sin_ref[rows, :], 1.0)
            turned[rows, j * head : (j + 1) * head] = rotated.astype(jnp.bfloat16)
        turned[rows, q_cols + head :] = projected[:, q_cols + head :].astype(jnp.bfloat16)

    each_rows(tokens, project)
    factor = head ** (-0.5)

    def attend_head(j, cols):
        for start, end in spans(tokens, 256):
            query = turned[start:end, cols]
            keys = turned[start:end, q_cols : q_cols + head]
            scores = contract_cols(query, keys)
            row = lax.broadcasted_iota(jnp.int32, scores.shape, 0)
            col = lax.broadcasted_iota(jnp.int32, scores.shape, 1)
            scores = jnp.where(row >= col, scores, -1e30)
            top = jnp.max(scores, -1, keepdims=True)
            if start:
                before = contract_cols(query, turned[:start, q_cols : q_cols + head])
                top = jnp.maximum(top, jnp.max(before, -1, keepdims=True))
            weight = jnp.exp2((scores - top) * (factor * LOG2E))
            norm = jnp.sum(weight, -1, keepdims=True)
            if start:
                weight_before = jnp.exp2((before - top) * (factor * LOG2E))
                norm = norm + jnp.sum(weight_before, -1, keepdims=True)
            inverse = 1.0 / norm
            total = dense(
                (weight * inverse).astype(jnp.bfloat16), turned[start:end, q_cols + head :]
            )
            if start:
                total = total + dense(
                    (weight_before * inverse).astype(jnp.bfloat16),
                    turned[:start, q_cols + head :],
                )
            mixed[start:end, cols] = total.astype(jnp.bfloat16)
            lse_ref[0, j, 0:1, start:end] = to_row(top * factor + jnp.log(norm))

    each_head(group, head, attend_head)


def fixed(shape):
    return pl.BlockSpec(
        shape, lambda i, off: (0,) * len(shape), pipeline_mode=pl.Buffered(buffer_count=1)
    )


ANYWHERE = pl.BlockSpec(memory_space=pl.ANY)


def params(limit=None):
    return pltpu.CompilerParams(
        dimension_semantics=("arbitrary",), vmem_limit_bytes=limit or 60 * 1024 * 1024
    )


def cost(flops, bytes_moved):
    return pl.CostEstimate(flops=int(flops), bytes_accessed=int(bytes_moved), transcendentals=0)


def attend_call(
    offsets, hidden, cos_two, sin_two, gains_t, pieces, inside, which, kv_local, group, head, kept
):
    tokens, width = hidden.shape
    cols = (group + 2) * head
    raw_cols = (group + 1) * head
    here = lambda i, off: (0, which)
    kept = tuple(kept or ())
    return pl.pallas_call(
        functools.partial(
            attend_kernel,
            inside=inside,
            pieces_count=len(pieces),
            group=group,
            head=head,
            eps=norm_eps,
        ),
        out_shape=(
            jax.ShapeDtypeStruct((tokens, kv_local * cols), jnp.bfloat16),
            jax.ShapeDtypeStruct((tokens, kv_local * raw_cols), jnp.float32),
            jax.ShapeDtypeStruct((tokens, kv_local * group * head), jnp.bfloat16),
            jax.ShapeDtypeStruct((kv_local, group, 8, tokens), jnp.float32),
        ),
        grid_spec=pltpu.PrefetchScalarGridSpec(
            num_scalar_prefetch=1,
            grid=(1,),
            in_specs=[
                fixed((tokens, width)),
                fixed((tokens, head)),
                fixed((tokens, head)),
                fixed((2, head)),
            ]
            + [ANYWHERE] * (len(pieces) + len(kept)),
            out_specs=(
                pl.BlockSpec((tokens, cols), here),
                pl.BlockSpec((tokens, raw_cols), here),
                pl.BlockSpec((tokens, group * head), here),
                pl.BlockSpec((1, group, 8, tokens), lambda i, off: (which, 0, 0, 0)),
            ),
            scratch_shapes=[
                pltpu.VMEM((width, cols), jnp.bfloat16),
                pltpu.SemaphoreType.DMA((lax.axis_size(DP),)),
            ],
        ),
        input_output_aliases={5 + len(pieces) + k: k for k in range(len(kept))},
        compiler_params=params(),
        cost_estimate=cost(
            2 * tokens * width * cols + 3 * tokens * tokens * head * group,
            tokens * (width * 2 + cols * 2 + raw_cols * 4 + group * head * 2) + width * cols * 2,
        ),
    )(offsets, hidden, cos_two, sin_two, gains_t, *pieces, *kept)


def project_kernel(offsets, *rest, parts):
    mixed, pieces, (out, weights, sems) = rest[:parts], rest[parts:-3], rest[-3:]
    copies = block_copies(pieces, weights, offsets, sems, None)
    for copy in copies:
        copy.start()
    for copy in copies:
        copy.wait()
    cols = mixed[0].shape[1]

    def project(rows):
        total = None
        for index, part in enumerate(mixed):
            term = contract_cols(part[rows, :], weights[:, index * cols : (index + 1) * cols])
            total = term if total is None else total + term
        out[rows, :] = total.astype(jnp.bfloat16)

    each_rows(mixed[0].shape[0], project)


def project_call(offsets, mixed, pieces):
    tokens, cols = mixed[0].shape
    width = pieces[0].shape[1] * lax.axis_size(DP)
    total_cols = cols * len(mixed)
    blocks = lax.axis_size(DP)
    return pl.pallas_call(
        functools.partial(project_kernel, parts=len(mixed)),
        out_shape=jax.ShapeDtypeStruct((tokens, width), jnp.bfloat16),
        grid_spec=pltpu.PrefetchScalarGridSpec(
            num_scalar_prefetch=1,
            grid=(1,),
            in_specs=[fixed((tokens, cols))] * len(mixed) + [ANYWHERE] * len(pieces),
            out_specs=fixed((tokens, width)),
            scratch_shapes=[
                pltpu.VMEM((width, total_cols), jnp.bfloat16),
                pltpu.SemaphoreType.DMA((blocks,)),
            ],
        ),
        compiler_params=params(),
        cost_estimate=cost(
            2 * tokens * width * total_cols,
            2 * tokens * (width + total_cols) + 2 * width * total_cols,
        ),
    )(offsets, *mixed, *pieces)


def feed_kernel(
    load_at, hidden, hidden_t, grad, grad_t, *rest, subs, size, first, last
):
    rest = list(rest)
    if first:
        outer_in = inner_in = None
    else:
        outer_in, inner_in = rest[:2]
        rest = rest[2:]
    count = len(rest) - 14
    pieces, (outer, inner), outs = rest[:count], rest[count : count + 2], rest[count + 2 : count + 6]
    weights, act, d_gate, d_up, total, outer_sum, inner_sum, sems = rest[count + 6 :]
    step = pl.program_id(0)
    tokens, width = hidden.shape

    @pl.when(step == 0)
    def _():
        for lead in range(subs):
            for copy in block_copies(pieces, weights, load_at, sems, lead):
                copy.start()
        outer_sum[...] = jnp.zeros_like(outer_sum) if first else outer_in[...]
        inner_sum[...] = jnp.zeros_like(inner_sum) if first else inner_in[...]

    for copy in block_copies(pieces, weights, load_at, sems, step):
        copy.wait()

    def forward(rows):
        gate = dense(hidden[rows, :], weights[step, :, :size])
        upper = dense(hidden[rows, :], weights[step, :, size : 2 * size])
        grad_act = dense(grad[rows, :], weights[step, :, 2 * size :])
        sigma = jax.nn.sigmoid(gate)
        silu = gate * sigma
        act[rows, :] = (silu * upper).astype(jnp.bfloat16)
        d_gate[rows, :] = (grad_act * upper * sigma * (1.0 + gate * (1.0 - sigma))).astype(
            jnp.bfloat16
        )
        d_up[rows, :] = (grad_act * silu).astype(jnp.bfloat16)
        outer_sum[rows, :] += contract_cols(act[rows, :], weights[step, :, 2 * size :])
        inner_sum[rows, :] += contract_cols(
            d_gate[rows, :], weights[step, :, :size]
        ) + contract_cols(d_up[rows, :], weights[step, :, size : 2 * size])

    each_rows(tokens, forward)

    def weight_rows(index, rows):
        total[rows, :size] = dense(hidden_t[rows, :], d_gate[...])
        total[rows, size : 2 * size] = dense(hidden_t[rows, :], d_up[...])
        total[rows, 2 * size :] = dense(grad_t[rows, :], act[...])

    each_head(width // 512, 512, weight_rows)
    store_blocks(total, outs, load_at, True)

    @pl.when(step == subs - 1)
    def _():
        outer[...] = outer_sum[...].astype(outer.dtype)
        inner[...] = inner_sum[...].astype(inner.dtype)


def fixed_two(shape):
    return pl.BlockSpec(
        shape, lambda i, a: (0,) * len(shape), pipeline_mode=pl.Buffered(buffer_count=1)
    )


def feed_call(load_at, hidden, hidden_t, grad, grad_t, sums, pieces, size, last):
    tokens, width = hidden.shape
    places, subs, rows, cols = pieces[0].shape
    blocks = lax.axis_size(DP)
    first = sums is None
    kind = jnp.bfloat16 if last else jnp.float32
    whole = fixed_two((tokens, width))
    turned = fixed_two((width, tokens))
    piece_spec = pl.BlockSpec((places, 1, rows, cols), lambda i, a: (0, i, 0, 0))
    result = pl.pallas_call(
        functools.partial(feed_kernel, subs=subs, size=size, first=first, last=last),
        out_shape=(
            jax.ShapeDtypeStruct((tokens, width), kind),
            jax.ShapeDtypeStruct((tokens, width), kind),
        )
        + (jax.ShapeDtypeStruct((places, subs, rows, cols), jnp.bfloat16),) * 4,
        grid_spec=pltpu.PrefetchScalarGridSpec(
            num_scalar_prefetch=1,
            grid=(subs,),
            in_specs=[whole, turned, whole, turned]
            + ([] if first else [whole, whole])
            + [ANYWHERE] * len(pieces),
            out_specs=(whole, whole) + (piece_spec,) * 4,
            scratch_shapes=[
                pltpu.VMEM((subs, width, cols), jnp.bfloat16),
                pltpu.VMEM((tokens, size), jnp.bfloat16),
                pltpu.VMEM((tokens, size), jnp.bfloat16),
                pltpu.VMEM((tokens, size), jnp.bfloat16),
                pltpu.VMEM((width, cols), jnp.float32),
                pltpu.VMEM((tokens, width), jnp.float32),
                pltpu.VMEM((tokens, width), jnp.float32),
                pltpu.SemaphoreType.DMA((subs, blocks)),
            ],
        ),
        compiler_params=params(),
        cost_estimate=cost(
            18 * tokens * width * size * subs,
            tokens * width * (8 + 16) + 4 * width * cols * subs,
        ),
    )(load_at, hidden, hidden_t, grad, grad_t, *(sums or ()), *pieces)
    return result[:2], list(result[2:])


def outer_kernel(load_at, grad, grad_t, mixed, *rest):
    pieces, mixed_grad, outs, (weights, total, sems) = rest[:-8], rest[-8], rest[-7:-3], rest[-3:]
    step = pl.program_id(0)
    block = mixed.shape[1]

    @pl.when(step == 0)
    def _():
        for copy in block_copies(pieces, weights, load_at, sems, None):
            copy.start()

    def weight_rows(index, rows):
        total[rows, :] = dense(grad_t[rows, :], mixed[...])

    each_head(grad_t.shape[0] // 512, 512, weight_rows)
    store_blocks(total, outs, load_at, True)

    @pl.when(step == 0)
    def _():
        for copy in block_copies(pieces, weights, load_at, sems, None):
            copy.wait()

    column = pl.ds(pl.multiple_of(step * block, block), block)

    def back_rows(rows):
        mixed_grad[rows, :] = dense(grad[rows, :], weights[:, column]).astype(jnp.bfloat16)

    each_rows(grad.shape[0], back_rows)


def outer_call(load_at, grad, grad_t, mixed, pieces, block, more):
    tokens, width = grad.shape
    cols = mixed.shape[1]
    places, rows, _ = pieces[0].shape
    subs = cols // block
    piece_spec = pl.BlockSpec((places, 1, rows, block), lambda i, a: (0, i, 0, 0))
    by_step = pl.BlockSpec((tokens, block), lambda i, a: (0, i))
    result = pl.pallas_call(
        outer_kernel,
        out_shape=(jax.ShapeDtypeStruct((tokens, cols), jnp.bfloat16),)
        + (jax.ShapeDtypeStruct((places, subs + more, rows, block), jnp.bfloat16),) * 4,
        grid_spec=pltpu.PrefetchScalarGridSpec(
            num_scalar_prefetch=1,
            grid=(subs,),
            in_specs=[fixed_two((tokens, width)), fixed_two((width, tokens)), by_step]
            + [ANYWHERE] * len(pieces),
            out_specs=(by_step,) + (piece_spec,) * 4,
            scratch_shapes=[
                pltpu.VMEM((width, cols), jnp.bfloat16),
                pltpu.VMEM((width, block), jnp.float32),
                pltpu.SemaphoreType.DMA((lax.axis_size(DP),)),
            ],
        ),
        compiler_params=params(),
        cost_estimate=cost(4 * tokens * width * cols, 4 * tokens * (width + cols) + 4 * width * cols),
    )(load_at, grad, grad_t, mixed, *pieces)
    return result[0], list(result[1:])


def back_kernel(
    load_at,
    hidden_t,
    cos_ref,
    sin_ref,
    gains,
    turned,
    raw,
    mixed,
    mixed_grad,
    lse_ref,
    *rest,
    kv_first,
    kv_count,
    sizes,
    per_group,
    group,
    head,
    eps,
    first,
    last,
):
    rest = list(rest)
    if first:
        sum_in = None
    else:
        sum_in = rest[0]
        rest = rest[1:]
    pieces = split_groups(rest, sizes)
    hidden_out, head_sum = rest[-14:-12]
    outs = rest[-12:-8]
    weights, d_query, d_key, d_value, d_all, total, hidden_sum, sems = rest[-8:]
    step = pl.program_id(0)
    tokens = raw.shape[0]
    width = hidden_t.shape[0]
    q_cols = group * head
    factor = head ** (-0.5)

    @pl.when(step == 0)
    def _():
        for lead in range(kv_count):
            for copy in head_copies(pieces, per_group, weights, load_at, sems, kv_first, lead):
                copy.start()
        head_sum[...] = jnp.zeros_like(head_sum)
        hidden_sum[...] = jnp.zeros_like(hidden_sum) if first else sum_in[...]

    d_key[...] = jnp.zeros_like(d_key)
    d_value[...] = jnp.zeros_like(d_value)

    def back_head(j, cols):
        for start, end in spans(tokens, 256):
            query = turned[start:end, cols]
            grad = mixed_grad[start:end, cols]
            delta = to_row(
                jnp.sum(
                    grad.astype(jnp.float32) * mixed[start:end, cols].astype(jnp.float32),
                    -1,
                    keepdims=True,
                )
            )
            shift = lse_ref[0, j, 0:1, start:end] * LOG2E
            grad_query = None
            for low, high in ((0, start), (start, end)):
                if low == high:
                    continue
                keys = turned[low:high, q_cols : q_cols + head]
                values = turned[low:high, q_cols + head :]
                scores = contract_cols(keys, query)
                probs = jnp.exp2(scores * (factor * LOG2E) - shift)
                if low == start:
                    probs = jnp.where(causal_t(0, high - low, 0, end - start), probs, 0.0)
                grad_probs = contract_cols(values, grad)
                grad_scores = (probs * (grad_probs - delta) * factor).astype(jnp.bfloat16)
                d_value[low:high, :] += dense(probs.astype(jnp.bfloat16), grad)
                d_key[low:high, :] += dense(grad_scores, query)
                term = contract_rows(grad_scores, keys)
                grad_query = term if grad_query is None else grad_query + term
            d_query[start:end, cols] = grad_query

    each_head(group, head, back_head)
    sums = [None, None]
    for j in range(group + 1):
        cols = slice(j * head, (j + 1) * head)
        which = 0 if j < group else 1
        for start, end in spans(tokens, 416):
            part = raw[start:end, cols]
            scale = lax.rsqrt(jnp.mean(part * part, -1, keepdims=True) + eps)
            normed = part * scale
            grad = d_query[start:end, cols] if j < group else d_key[start:end, :]
            grad = rotate_rows(grad, cos_ref[start:end, :], sin_ref[start:end, :], -1.0)
            product = jnp.sum(grad * normed, 0, keepdims=True)
            sums[which] = product if sums[which] is None else sums[which] + product
            grad = grad * gains[which : which + 1, :]
            d_all[start:end, cols] = (
                scale * (grad - normed * jnp.mean(grad * normed, -1, keepdims=True))
            ).astype(jnp.bfloat16)
    head_sum[0:1, :] += sums[0]
    head_sum[1:2, :] += sums[1]
    d_all[:, q_cols + head :] = d_value[...].astype(jnp.bfloat16)

    def weight_rows(index, rows):
        total[rows, :] = dense(hidden_t[rows, :], d_all[...])

    each_head(width // 512, 512, weight_rows)
    store_blocks(total, outs, load_at, True)
    for lead in range(kv_count):

        @pl.when(step == lead)
        def _():
            for copy in head_copies(pieces, per_group, weights, load_at, sems, kv_first, lead):
                copy.wait()

    def hidden_rows(rows):
        hidden_sum[rows, :] += contract_cols(d_all[rows, :], weights[step])

    each_rows(tokens, hidden_rows)

    @pl.when(step == kv_count - 1)
    def _():
        hidden_out[...] = hidden_sum[...].astype(hidden_out.dtype)


def head_copies(groups, per_group, buffer, offsets, sems, kv_first, lead):
    pieces = groups[(kv_first + lead) // per_group]
    inside = (kv_first + lead) % per_group
    rows = pieces[0].shape[-2]
    copies = []
    index = 0
    for piece in pieces:
        for place in range(piece.shape[0]):
            start = pl.multiple_of(offsets[index] * rows, rows)
            copies.append(
                pltpu.make_async_copy(
                    piece.at[place, inside],
                    buffer.at[lead, pl.ds(start, rows), :],
                    sems.at[lead, index],
                )
            )
            index += 1
    return copies


def split_groups(refs, sizes):
    groups = []
    for size in sizes:
        groups.append(refs[:size])
        refs = refs[size:]
    return groups


def back_call(
    load_at,
    hidden_t,
    tables,
    kept,
    mixed_grad,
    sum_in,
    groups,
    kv_first,
    kv_count,
    group,
    head,
    last,
    into,
):
    cos_two, sin_two, gains_t = tables
    turned, raw, mixed, lse_t = kept
    width, tokens = hidden_t.shape
    cols = (group + 2) * head
    raw_cols = (group + 1) * head
    pieces = [piece for one in groups for piece in one]
    places, per_group, rows, _ = pieces[0].shape
    blocks = lax.axis_size(DP)
    first = sum_in is None
    by_step = lambda i, a: (0, kv_first + i)
    into = list(into or ())
    subs = into[0].shape[1] if into else kv_count
    shift = subs - kv_count
    ahead = 10 + (0 if first else 1) + len(pieces)
    whole = fixed_two((tokens, width))
    result = pl.pallas_call(
        functools.partial(
            back_kernel,
            kv_first=kv_first,
            kv_count=kv_count,
            sizes=tuple(len(one) for one in groups),
            per_group=per_group,
            group=group,
            head=head,
            eps=norm_eps,
            first=first,
            last=last,
        ),
        out_shape=(
            jax.ShapeDtypeStruct((tokens, width), jnp.bfloat16 if last else jnp.float32),
            jax.ShapeDtypeStruct((8, head), jnp.float32),
        )
        + (jax.ShapeDtypeStruct((places, subs, rows, cols), jnp.bfloat16),) * 4,
        grid_spec=pltpu.PrefetchScalarGridSpec(
            num_scalar_prefetch=1,
            grid=(kv_count,),
            in_specs=[
                fixed_two((width, tokens)),
                fixed_two((tokens, head)),
                fixed_two((tokens, head)),
                fixed_two((2, head)),
                pl.BlockSpec((tokens, cols), by_step),
                pl.BlockSpec((tokens, raw_cols), by_step),
                pl.BlockSpec((tokens, group * head), by_step),
                pl.BlockSpec((tokens, group * head), by_step),
                pl.BlockSpec((1, group, 8, tokens), lambda i, a: (kv_first + i, 0, 0, 0)),
            ]
            + ([] if first else [whole])
            + [ANYWHERE] * (len(pieces) + len(into)),
            out_specs=(whole, fixed_two((8, head)))
            + (pl.BlockSpec((places, 1, rows, cols), lambda i, a: (0, shift + i, 0, 0)),) * 4,
            scratch_shapes=[
                pltpu.VMEM((kv_count, width, cols), jnp.bfloat16),
                pltpu.VMEM((tokens, group * head), jnp.float32),
                pltpu.VMEM((tokens, head), jnp.float32),
                pltpu.VMEM((tokens, head), jnp.float32),
                pltpu.VMEM((tokens, cols), jnp.bfloat16),
                pltpu.VMEM((width, cols), jnp.float32),
                pltpu.VMEM((tokens, width), jnp.float32),
                pltpu.SemaphoreType.DMA((kv_count, blocks)),
            ],
        ),
        input_output_aliases={ahead + k: 2 + k for k in range(len(into))},
        compiler_params=params(),
        cost_estimate=cost(
            4 * tokens * width * cols * kv_count + 7 * tokens * tokens * head * group * kv_count,
            tokens * (width * 6 + kv_count * (cols * 2 + raw_cols * 4 + group * head * 4))
            + width * cols * kv_count * 4,
        ),
    )(
        load_at,
        hidden_t,
        cos_two,
        sin_two,
        gains_t,
        turned,
        raw,
        mixed,
        mixed_grad,
        lse_t,
        *(() if first else (sum_in,)),
        *pieces,
        *into,
    )
    return result[0], result[1], list(result[2:])


def adam(param, grad, first, second, rate, decay):
    new_first = 0.9 * first + 0.1 * grad
    new_second = 0.95 * second + 0.05 * grad * grad
    fix_first = 1.0 - 0.9**ADAM_STEP
    fix_second = 1.0 - 0.95**ADAM_STEP
    step_size = new_first / fix_first / (jnp.sqrt(new_second / fix_second) + 1e-08)
    return (param - rate * (step_size + decay * param), new_first, new_second)


def own_rows(full, count):
    return lax.dynamic_slice_in_dim(full, lax.axis_index(DP) * count, count, 0)


def local(
    block_in,
    grad_out,
    query_weight,
    keyvalue_matrix,
    output_weight,
    feedfwd_weight,
    norm_gains,
    head_gains,
    first_query,
    keyvalue_first_moment,
    first_output,
    first_feedfwd,
    first_norm,
    first_head,
    second_query,
    keyvalue_second_moment,
    second_output,
    second_feedfwd,
    second_norm,
    second_head,
):
    tokens = block_in.shape[0]
    width = block_in.shape[1]
    head_size = head_gains.shape[0]
    group = QUERY_HEADS // KEYVALUE_HEADS
    keyvalue_columns = keyvalue_matrix.shape[2]
    kv_local = keyvalue_columns // head_size
    ffn_local = feedfwd_weight.shape[2]
    q_cols = group * head_size
    half_type = jnp.bfloat16
    grad_scale = float(tokens * lax.axis_size(DP)) ** (-0.5)
    load_at = block_places()
    size = 256 if ffn_local % 512 == 0 else 128
    per_call = 2 if ffn_local % (2 * size) == 0 else 1
    if ffn_local // (per_call * size) > 3 or ffn_local % (per_call * size):
        per_call = ffn_local // size
    calls = ffn_local // (per_call * size)

    packed = jnp.stack(
        [
            jnp.concatenate(
                [
                    query_weight[:, n * q_cols : (n + 1) * q_cols],
                    keyvalue_matrix[:, 0, n * head_size : (n + 1) * head_size],
                    keyvalue_matrix[:, 1, n * head_size : (n + 1) * head_size],
                ],
                1,
            ).astype(half_type)
            for n in range(kv_local)
        ]
    )
    feed_parts = []
    for c in range(calls):
        blocks = []
        for b in range(c * per_call, (c + 1) * per_call):
            blocks.append(
                jnp.concatenate(
                    [feedfwd_weight[:, t, b * size : (b + 1) * size] for t in range(3)], 1
                ).astype(half_type)
            )
        feed_parts.append(jnp.stack(blocks))
    per_group = 2 if kv_local % 2 == 0 else kv_local
    qkv_pieces = [
        plane_gather(line_gather(packed[c * per_group : (c + 1) * per_group]), BOTH)
        for c in range(kv_local // per_group)
    ]
    out_pieces = plane_gather(line_gather(output_weight.astype(half_type)), BOTH)
    feed_pieces = [plane_gather(line_gather(part), BOTH) for part in feed_parts]

    gains_two = norm_gains.T
    tables = rot_table(tokens, head_size) + (head_gains.T,)
    full = jnp.float32
    hidden_one, hidden_one_t, grad_out_t = row_call(
        prepare_kernel,
        (block_in, grad_out, gains_two),
        (("r", half_type), ("t", half_type), ("t", half_type)),
        10,
    )
    kept = None
    for c in range(kv_local):
        kept = attend_call(
            load_at,
            hidden_one,
            *tables,
            qkv_pieces[c // per_group],
            c % per_group,
            c,
            kv_local,
            group,
            head_size,
            kept,
        )
    mixed = kept[2]
    attn_half = project_call(load_at, [mixed], out_pieces)
    resid, hidden_two, hidden_two_t = row_call(
        middle_kernel,
        (block_in, *tensor_terms(attn_half), gains_two),
        (("r", full), ("r", half_type), ("t", half_type)),
        14,
    )

    sums = None
    feed_rows = []
    for c in range(calls):
        sums, grads = feed_call(
            load_at,
            hidden_two,
            hidden_two_t,
            grad_out,
            grad_out_t,
            sums,
            feed_pieces[c],
            size,
            c == calls - 1,
        )
        feed_rows.append(plane_sum(grads, SECOND if c % 2 == 0 else FIRST))
    ffn_half, grad_hidden_half = sums
    grad_resid, grad_resid_half, grad_resid_half_t, gain_two = row_call(
        functools.partial(late_kernel, tokens=tokens),
        (resid, grad_out, *tensor_terms(grad_hidden_half), gains_two),
        (("r", full), ("r", half_type), ("t", half_type), ("s", full)),
        18,
    )
    left, right = tensor_terms(ffn_half)
    block_out = (resid + (left.astype(full) + right.astype(full))).astype(half_type)
    columns = (group + 2) * head_size
    block = columns if mixed.shape[1] % columns == 0 else mixed.shape[1]
    mixed_gradient, grads = outer_call(
        load_at,
        grad_resid_half,
        grad_resid_half_t,
        mixed,
        out_pieces,
        block,
        0,
    )
    output_blocks = plane_sum(grads, FIRST)
    hidden_part = None
    head_part = None
    packed_rows = []
    for start in range(0, kv_local, per_group):
        count = per_group
        hidden_part, heads, grads = back_call(
            load_at,
            hidden_one_t,
            tables,
            kept,
            mixed_gradient,
            hidden_part,
            qkv_pieces,
            start,
            count,
            group,
            head_size,
            start + count == kv_local,
            None,
        )
        head_part = heads if head_part is None else head_part + heads
        rows_sum = plane_sum(grads, SECOND)
        packed_rows.append(rows_sum)
    by_block = line_sum(feed_rows[:1])
    if calls > 1:
        by_block += line_sum(feed_rows[1:])
    (output_rows,) = line_sum([output_blocks])
    by_head = []
    for part in packed_rows:
        by_head += line_sum([part])
    output_rows = jnp.concatenate(list(output_rows), 1)
    grad_input, gain_one = row_call(
        functools.partial(final_kernel, tokens=tokens),
        (block_in, grad_resid, *tensor_terms(hidden_part), gains_two),
        (("r", half_type), ("s", full)),
        12,
    )
    left, right = tensor_terms(head_part[:2].astype(half_type))
    head_both = left.astype(full) + right.astype(full)
    small = jnp.concatenate(
        [gain_one[0].reshape(-1, 128), gain_two[0].reshape(-1, 128), head_both.reshape(-1, 128)]
    )
    small = all_sum_small(small)
    lanes = width // 128
    grad_norm = jnp.stack(
        [small[:lanes].reshape(width), small[lanes : 2 * lanes].reshape(width)], 1
    )
    grad_head = small[2 * lanes :].reshape(2, head_size).T
    norm_rows = own_rows(grad_norm, first_norm.shape[0]) * grad_scale
    head_rows = own_rows(grad_head, first_head.shape[0]) * grad_scale

    by_head = jnp.concatenate(by_head)
    query_rows = jnp.concatenate([by_head[n, :, :q_cols] for n in range(kv_local)], 1) * grad_scale
    keyvalue_rows = (
        jnp.stack(
            [
                jnp.concatenate(
                    [
                        by_head[n, :, q_cols + t * head_size : q_cols + (t + 1) * head_size]
                        for n in range(kv_local)
                    ],
                    1,
                )
                for t in range(2)
            ],
            1,
        )
        * grad_scale
    )
    output_rows = output_rows * grad_scale
    by_block = jnp.concatenate(by_block)
    feedfwd_grad_rows = (
        jnp.stack(
            [
                jnp.concatenate(
                    [
                        by_block[b, :, t * size : (t + 1) * size]
                        for b in range(ffn_local // size)
                    ],
                    1,
                )
                for t in range(3)
            ],
            1,
        )
        * grad_scale
    )
    norm_own = own_rows(norm_gains, first_norm.shape[0])
    head_own = own_rows(head_gains, first_head.shape[0])
    new_query, new_first_query, new_second_query = adam(
        query_weight, query_rows, first_query, second_query, 0.01, 0.1
    )
    new_keyvalue, new_first_keyvalue, new_second_keyvalue = adam(
        keyvalue_matrix, keyvalue_rows, keyvalue_first_moment, keyvalue_second_moment, 0.01, 0.1
    )
    new_output, new_first_output, new_second_output = adam(
        output_weight, output_rows, first_output, second_output, 0.01, 0.1
    )
    new_feedfwd, new_first_feedfwd, new_second_feedfwd = adam(
        feedfwd_weight, feedfwd_grad_rows, first_feedfwd, second_feedfwd, 0.01, 0.1
    )
    new_norm, new_first_norm, new_second_norm = adam(
        norm_own, norm_rows, first_norm, second_norm, 0.1, 0.0
    )
    new_head, new_first_head, new_second_head = adam(
        head_own, head_rows, first_head, second_head, 0.1, 0.0
    )
    return (
        block_out,
        grad_input,
        query_rows,
        keyvalue_rows,
        output_rows,
        feedfwd_grad_rows,
        norm_rows,
        head_rows,
        new_query,
        new_keyvalue,
        new_output,
        new_feedfwd,
        new_norm,
        new_head,
        new_first_query,
        new_first_keyvalue,
        new_first_output,
        new_first_feedfwd,
        new_first_norm,
        new_first_head,
        new_second_query,
        new_second_keyvalue,
        new_second_output,
        new_second_feedfwd,
        new_second_norm,
        new_second_head,
    )


def solution(mesh):
    placed = (
        ROWS,
        ROWS,
        FLAT,
        DEEP,
        FLAT,
        DEEP,
        P(),
        P(),
        FLAT,
        DEEP,
        FLAT,
        DEEP,
        ROWS,
        ROWS,
        FLAT,
        DEEP,
        FLAT,
        DEEP,
        ROWS,
        ROWS,
    )
    return jax.shard_map(
        local,
        mesh=mesh,
        in_specs=placed,
        out_specs=(
            ROWS,
            ROWS,
            FLAT,
            DEEP,
            FLAT,
            DEEP,
            ROWS,
            ROWS,
            FLAT,
            DEEP,
            FLAT,
            DEEP,
            ROWS,
            ROWS,
            FLAT,
            DEEP,
            FLAT,
            DEEP,
            ROWS,
            ROWS,
            FLAT,
            DEEP,
            FLAT,
            DEEP,
            ROWS,
            ROWS,
        ),
        check_vma=False,
    )
```

```python
import functools

import jax
import jax.numpy as jnp
from jax import lax
from jax.experimental import pallas as pl
from jax.experimental.pallas import tpu as pltpu
from jax.sharding import PartitionSpec as P


QUERY_HEADS = 16
KEYVALUE_HEADS = 8
ADAM_STEP = 2


DP, TP = "dp", "tensor"
ROWS, FLAT, DEEP = P(DP, None), P(DP, TP), P(DP, None, TP)
FIRST, SECOND, BOTH = "first", "second", "both"
norm_eps = 1e-06
rope_base = 1000000.0


def rope_tables(length, head):
    half = head // 2
    freq = rope_base ** (-2.0 * jnp.arange(half, dtype=jnp.float32) / head)
    angle = jnp.arange(length, dtype=jnp.float32)[:, None] * freq[None, :]
    return (jnp.cos(angle), jnp.sin(angle))


def rms_scale(values):
    return lax.rsqrt(jnp.mean(values * values, -1, keepdims=True) + norm_eps)


def norm_back(grad_normed, normed, scale):
    return scale * (grad_normed - normed * jnp.mean(grad_normed * normed, -1, keepdims=True))


def dense(left, right):
    return jnp.dot(left, right, preferred_element_type=jnp.float32)


def contract_cols(left, right):
    return lax.dot_general(
        left, right, (((1,), (1,)), ((), ())), preferred_element_type=jnp.float32
    )


def contract_rows(left, right):
    return lax.dot_general(
        left, right, (((0,), (0,)), ((), ())), preferred_element_type=jnp.float32
    )


def rot_table(tokens, head):
    cosine, sine = rope_tables(tokens, head)
    return jnp.concatenate([cosine, cosine], 1), jnp.concatenate([-sine, sine], 1)


def peer_exchange(values):
    return lax.ppermute(values, TP, [(0, 1), (1, 0)])


def tensor_terms(partial):
    if lax.axis_size(TP) == 2:
        return partial, peer_exchange(partial)
    return lax.psum(partial, TP), jnp.zeros_like(partial)


def hop(values, flip):
    size = lax.axis_size(DP)
    return lax.ppermute(values, DP, [(i, i ^ flip) for i in range(size)])


def line_length():
    return lax.axis_size(DP) // 4


def block_places():
    steps = jnp.arange(line_length(), dtype=jnp.int32) * 4
    return lax.axis_index(DP) ^ jnp.concatenate([steps + flip for flip in range(4)])


def line_gather(values):
    return [values] + [hop(values, 4 * step) for step in range(1, line_length())]


def plane_gather(parts, way):
    own = jnp.stack(parts)
    first, second = hop(own, 1), hop(own, 2)
    if way == BOTH:
        cut = len(parts) // 2
        both = [hop(first[:cut], 2), hop(second[cut:], 1)]
    elif way == SECOND:
        both = [hop(first, 2)]
    else:
        both = [hop(second, 1)]
    return [own, first, second] + both


def add_half(left, right):
    return (left.astype(jnp.float32) + right.astype(jnp.float32)).astype(jnp.bfloat16)


def plane_sum(groups, way):
    own, first, second, both = groups
    cut = line_length() // 2
    if way == BOTH:
        low, high = hop(both[:cut], 2), hop(both[cut:], 1)
        first = jnp.concatenate([add_half(first[:cut], low), first[cut:]])
        second = jnp.concatenate([second[:cut], add_half(second[cut:], high)])
    elif way == SECOND:
        first = add_half(first, hop(both, 2))
    else:
        second = add_half(second, hop(both, 1))
    terms = [own, hop(first, 1), hop(second, 2)]
    return [
        sum(term[step].astype(jnp.float32) for term in terms) for step in range(line_length())
    ]


def line_sum(parts):
    arrived = [
        hop(jnp.concatenate([part[step].astype(jnp.bfloat16) for part in parts]), 4 * step)
        for step in range(1, line_length())
    ]
    results = []
    start = 0
    for part in parts:
        end = start + part[0].shape[0]
        total = part[0]
        for block in arrived:
            total = total + block[start:end].astype(jnp.float32)
        results.append(total)
        start = end
    return results


def all_sum_small(values):
    flip = 1
    while flip < lax.axis_size(DP):
        values = values + hop(values, flip)
        flip *= 2
    return values


def prepare_kernel(inputs, grad, gains, hidden, hidden_t, grad_t):
    values = inputs[...].astype(jnp.float32)
    normed = values * rms_scale(values)
    result = (normed * gains[0:1, :]).astype(jnp.bfloat16)
    hidden[...] = result
    hidden_t[...] = result.T
    grad_t[...] = grad[...].T


def middle_kernel(inputs, left, right, gains, resid, hidden, hidden_t):
    attn = left[...].astype(jnp.float32) + right[...].astype(jnp.float32)
    total = inputs[...].astype(jnp.float32) + attn
    resid[...] = total
    result = (total * rms_scale(total) * gains[1:2, :]).astype(jnp.bfloat16)
    hidden[...] = result
    hidden_t[...] = result.T


def gain_rows(product, gain, tokens):
    step = pl.program_id(0)
    row = lax.broadcasted_iota(jnp.int32, product.shape, 0) + step * product.shape[0]
    product = jnp.where(row < tokens, product, 0.0)

    @pl.when(step == 0)
    def _():
        gain[...] = jnp.zeros_like(gain)

    gain[0:1, :] += jnp.sum(product, 0, keepdims=True)


def late_kernel(resid, grad, left, right, gains, result, half, half_t, gain, *, tokens):
    total = resid[...]
    scale = rms_scale(total)
    normed = total * scale
    grad_hidden = left[...].astype(jnp.float32) + right[...].astype(jnp.float32)
    gain_rows(grad_hidden * normed, gain, tokens)
    grad_resid = grad[...].astype(jnp.float32) + norm_back(
        grad_hidden * gains[1:2, :], normed, scale
    )
    result[...] = grad_resid
    rounded = grad_resid.astype(jnp.bfloat16)
    half[...] = rounded
    half_t[...] = rounded.T


def final_kernel(inputs, grad_resid, left, right, gains, result, gain, *, tokens):
    values = inputs[...].astype(jnp.float32)
    scale = rms_scale(values)
    normed = values * scale
    grad_hidden = left[...].astype(jnp.float32) + right[...].astype(jnp.float32)
    gain_rows(grad_hidden * normed, gain, tokens)
    result[...] = (
        grad_resid[...] + norm_back(grad_hidden * gains[0:1, :], normed, scale)
    ).astype(jnp.bfloat16)


def row_call(kernel, ins, outs, moved):
    tokens, width = ins[0].shape
    block = 256
    specs = {
        "r": pl.BlockSpec((block, width), lambda i: (i, 0)),
        "t": pl.BlockSpec((width, block), lambda i: (0, i)),
        "g": pl.BlockSpec((2, width), lambda i: (0, 0)),
        "s": pl.BlockSpec((8, width), lambda i: (0, 0)),
    }
    shapes = {"r": (tokens, width), "t": (width, tokens), "s": (8, width)}
    return pl.pallas_call(
        kernel,
        out_shape=tuple(jax.ShapeDtypeStruct(shapes[kind], dtype) for kind, dtype in outs),
        grid=(pl.cdiv(tokens, block),),
        in_specs=[specs["g" if value.shape[0] == 2 else "r"] for value in ins],
        out_specs=tuple(specs[kind] for kind, _ in outs),
        compiler_params=params(),
        cost_estimate=cost(20 * tokens * width, moved * tokens * width),
    )(*ins)


def block_copies(pieces, buffer, offsets, sems, lead):
    rows = pieces[0].shape[-2]
    copies = []
    index = 0
    for piece in pieces:
        for place in range(piece.shape[0]):
            start = pl.multiple_of(offsets[index] * rows, rows)
            source = piece.at[place] if lead is None else piece.at[place, lead]
            target = buffer if lead is None else buffer.at[lead]
            sem = sems.at[index] if lead is None else sems.at[lead, index]
            copies.append(pltpu.make_async_copy(source, target.at[pl.ds(start, rows), :], sem))
            index += 1
    return copies


def store_blocks(total, outs, offsets, lead):
    index = 0
    for out in outs:
        rows = out.shape[-2]
        for place in range(out.shape[0]):
            start = pl.multiple_of(offsets[index] * rows, rows)
            block = total[pl.ds(start, rows), :].astype(jnp.bfloat16)
            if lead:
                out[place, 0] = block
            else:
                out[place] = block
            index += 1


def spans(size, step):
    return [(start, min(start + step, size)) for start in range(0, size, step)]


def each_rows(size, body):
    step = 416 if size % 416 == 0 else size
    for start in range(0, size, step):
        body(slice(start, start + step))


def each_head(count, head, body):
    for index in range(count):
        body(index, slice(index * head, (index + 1) * head))


def rotate_rows(values, cos_ref, sin_ref, sign):
    turned = pltpu.roll(values, values.shape[1] // 2, 1)
    return values * cos_ref + sign * turned * sin_ref


def to_row(column):
    return jnp.broadcast_to(column, (column.shape[0], 128)).T[0:1, :]


def causal_t(first_key, keys, first_query, queries):
    key = lax.broadcasted_iota(jnp.int32, (keys, queries), 0) + first_key
    query = lax.broadcasted_iota(jnp.int32, (keys, queries), 1) + first_query
    return key <= query


LOG2E = 1.4426950408889634


def attend_kernel(
    offsets, hidden, cos_ref, sin_ref, gains, *rest, inside, pieces_count, group, head, eps
):
    pieces, (turned, raw, mixed, lse_ref, weights, sems) = rest[:pieces_count], rest[-6:]
    tokens = hidden.shape[0]
    q_cols = group * head
    rows = pieces[0].shape[-2]
    copies = []
    for piece in pieces:
        for place in range(piece.shape[0]):
            index = len(copies)
            start = pl.multiple_of(offsets[index] * rows, rows)
            copies.append(
                pltpu.make_async_copy(
                    piece.at[place, inside], weights.at[pl.ds(start, rows), :], sems.at[index]
                )
            )
    for copy in copies:
        copy.start()
    for copy in copies:
        copy.wait()

    def project(rows):
        projected = dense(hidden[rows, :], weights[...])
        raw[rows, :] = projected[:, : q_cols + head]
        for j in range(group + 1):
            part = projected[:, j * head : (j + 1) * head]
            scale = lax.rsqrt(jnp.mean(part * part, -1, keepdims=True) + eps)
            gain = gains[0:1, :] if j < group else gains[1:2, :]
            rotated = rotate_rows(part * scale * gain, cos_ref[rows, :], sin_ref[rows, :], 1.0)
            turned[rows, j * head : (j + 1) * head] = rotated.astype(jnp.bfloat16)
        turned[rows, q_cols + head :] = projected[:, q_cols + head :].astype(jnp.bfloat16)

    each_rows(tokens, project)
    factor = head ** (-0.5)

    def attend_head(j, cols):
        for start, end in spans(tokens, 256):
            query = turned[start:end, cols]
            keys = turned[start:end, q_cols : q_cols + head]
            scores = contract_cols(query, keys)
            row = lax.broadcasted_iota(jnp.int32, scores.shape, 0)
            col = lax.broadcasted_iota(jnp.int32, scores.shape, 1)
            scores = jnp.where(row >= col, scores, -1e30)
            top = jnp.max(scores, -1, keepdims=True)
            if start:
                before = contract_cols(query, turned[:start, q_cols : q_cols + head])
                top = jnp.maximum(top, jnp.max(before, -1, keepdims=True))
            weight = jnp.exp2((scores - top) * (factor * LOG2E))
            norm = jnp.sum(weight, -1, keepdims=True)
            if start:
                weight_before = jnp.exp2((before - top) * (factor * LOG2E))
                norm = norm + jnp.sum(weight_before, -1, keepdims=True)
            inverse = 1.0 / norm
            total = dense(
                (weight * inverse).astype(jnp.bfloat16), turned[start:end, q_cols + head :]
            )
            if start:
                total = total + dense(
                    (weight_before * inverse).astype(jnp.bfloat16),
                    turned[:start, q_cols + head :],
                )
            mixed[start:end, cols] = total.astype(jnp.bfloat16)
            lse_ref[0, j, 0:1, start:end] = to_row(top * factor + jnp.log(norm))

    each_head(group, head, attend_head)


def fixed(shape):
    return pl.BlockSpec(
        shape, lambda i, off: (0,) * len(shape), pipeline_mode=pl.Buffered(buffer_count=1)
    )


ANYWHERE = pl.BlockSpec(memory_space=pl.ANY)


def params(limit=None):
    return pltpu.CompilerParams(
        dimension_semantics=("arbitrary",), vmem_limit_bytes=limit or 60 * 1024 * 1024
    )


def cost(flops, bytes_moved):
    return pl.CostEstimate(flops=int(flops), bytes_accessed=int(bytes_moved), transcendentals=0)


def attend_call(
    offsets, hidden, cos_two, sin_two, gains_t, pieces, inside, which, kv_local, group, head, kept
):
    tokens, width = hidden.shape
    cols = (group + 2) * head
    raw_cols = (group + 1) * head
    here = lambda i, off: (0, which)
    kept = tuple(kept or ())
    return pl.pallas_call(
        functools.partial(
            attend_kernel,
            inside=inside,
            pieces_count=len(pieces),
            group=group,
            head=head,
            eps=norm_eps,
        ),
        out_shape=(
            jax.ShapeDtypeStruct((tokens, kv_local * cols), jnp.bfloat16),
            jax.ShapeDtypeStruct((tokens, kv_local * raw_cols), jnp.float32),
            jax.ShapeDtypeStruct((tokens, kv_local * group * head), jnp.bfloat16),
            jax.ShapeDtypeStruct((kv_local, group, 8, tokens), jnp.float32),
        ),
        grid_spec=pltpu.PrefetchScalarGridSpec(
            num_scalar_prefetch=1,
            grid=(1,),
            in_specs=[
                fixed((tokens, width)),
                fixed((tokens, head)),
                fixed((tokens, head)),
                fixed((2, head)),
            ]
            + [ANYWHERE] * (len(pieces) + len(kept)),
            out_specs=(
                pl.BlockSpec((tokens, cols), here),
                pl.BlockSpec((tokens, raw_cols), here),
                pl.BlockSpec((tokens, group * head), here),
                pl.BlockSpec((1, group, 8, tokens), lambda i, off: (which, 0, 0, 0)),
            ),
            scratch_shapes=[
                pltpu.VMEM((width, cols), jnp.bfloat16),
                pltpu.SemaphoreType.DMA((lax.axis_size(DP),)),
            ],
        ),
        input_output_aliases={5 + len(pieces) + k: k for k in range(len(kept))},
        compiler_params=params(),
        cost_estimate=cost(
            2 * tokens * width * cols + 3 * tokens * tokens * head * group,
            tokens * (width * 2 + cols * 2 + raw_cols * 4 + group * head * 2) + width * cols * 2,
        ),
    )(offsets, hidden, cos_two, sin_two, gains_t, *pieces, *kept)


def project_kernel(offsets, *rest, parts):
    mixed, pieces, (out, weights, sems) = rest[:parts], rest[parts:-3], rest[-3:]
    copies = block_copies(pieces, weights, offsets, sems, None)
    for copy in copies:
        copy.start()
    for copy in copies:
        copy.wait()
    cols = mixed[0].shape[1]

    def project(rows):
        total = None
        for index, part in enumerate(mixed):
            term = contract_cols(part[rows, :], weights[:, index * cols : (index + 1) * cols])
            total = term if total is None else total + term
        out[rows, :] = total.astype(jnp.bfloat16)

    each_rows(mixed[0].shape[0], project)


def project_call(offsets, mixed, pieces):
    tokens, cols = mixed[0].shape
    width = pieces[0].shape[1] * lax.axis_size(DP)
    total_cols = cols * len(mixed)
    blocks = lax.axis_size(DP)
    return pl.pallas_call(
        functools.partial(project_kernel, parts=len(mixed)),
        out_shape=jax.ShapeDtypeStruct((tokens, width), jnp.bfloat16),
        grid_spec=pltpu.PrefetchScalarGridSpec(
            num_scalar_prefetch=1,
            grid=(1,),
            in_specs=[fixed((tokens, cols))] * len(mixed) + [ANYWHERE] * len(pieces),
            out_specs=fixed((tokens, width)),
            scratch_shapes=[
                pltpu.VMEM((width, total_cols), jnp.bfloat16),
                pltpu.SemaphoreType.DMA((blocks,)),
            ],
        ),
        compiler_params=params(),
        cost_estimate=cost(
            2 * tokens * width * total_cols,
            2 * tokens * (width + total_cols) + 2 * width * total_cols,
        ),
    )(offsets, *mixed, *pieces)


def feed_kernel(
    load_at, hidden, hidden_t, grad, grad_t, *rest, subs, size, first, last
):
    rest = list(rest)
    if first:
        outer_in = inner_in = None
    else:
        outer_in, inner_in = rest[:2]
        rest = rest[2:]
    count = len(rest) - 14
    pieces, (outer, inner), outs = rest[:count], rest[count : count + 2], rest[count + 2 : count + 6]
    weights, act, d_gate, d_up, total, outer_sum, inner_sum, sems = rest[count + 6 :]
    step = pl.program_id(0)
    tokens, width = hidden.shape

    @pl.when(step == 0)
    def _():
        for lead in range(subs):
            for copy in block_copies(pieces, weights, load_at, sems, lead):
                copy.start()
        outer_sum[...] = jnp.zeros_like(outer_sum) if first else outer_in[...]
        inner_sum[...] = jnp.zeros_like(inner_sum) if first else inner_in[...]

    for copy in block_copies(pieces, weights, load_at, sems, step):
        copy.wait()

    def forward(rows):
        gate = dense(hidden[rows, :], weights[step, :, :size])
        upper = dense(hidden[rows, :], weights[step, :, size : 2 * size])
        grad_act = dense(grad[rows, :], weights[step, :, 2 * size :])
        sigma = jax.nn.sigmoid(gate)
        silu = gate * sigma
        act[rows, :] = (silu * upper).astype(jnp.bfloat16)
        d_gate[rows, :] = (grad_act * upper * sigma * (1.0 + gate * (1.0 - sigma))).astype(
            jnp.bfloat16
        )
        d_up[rows, :] = (grad_act * silu).astype(jnp.bfloat16)
        outer_sum[rows, :] += contract_cols(act[rows, :], weights[step, :, 2 * size :])
        inner_sum[rows, :] += contract_cols(
            d_gate[rows, :], weights[step, :, :size]
        ) + contract_cols(d_up[rows, :], weights[step, :, size : 2 * size])

    each_rows(tokens, forward)

    def weight_rows(index, rows):
        total[rows, :size] = dense(hidden_t[rows, :], d_gate[...])
        total[rows, size : 2 * size] = dense(hidden_t[rows, :], d_up[...])
        total[rows, 2 * size :] = dense(grad_t[rows, :], act[...])

    each_head(width // 512, 512, weight_rows)
    store_blocks(total, outs, load_at, True)

    @pl.when(step == subs - 1)
    def _():
        outer[...] = outer_sum[...].astype(outer.dtype)
        inner[...] = inner_sum[...].astype(inner.dtype)


def fixed_two(shape):
    return pl.BlockSpec(
        shape, lambda i, a: (0,) * len(shape), pipeline_mode=pl.Buffered(buffer_count=1)
    )


def feed_call(load_at, hidden, hidden_t, grad, grad_t, sums, pieces, size, last):
    tokens, width = hidden.shape
    places, subs, rows, cols = pieces[0].shape
    blocks = lax.axis_size(DP)
    first = sums is None
    kind = jnp.bfloat16 if last else jnp.float32
    whole = fixed_two((tokens, width))
    turned = fixed_two((width, tokens))
    piece_spec = pl.BlockSpec((places, 1, rows, cols), lambda i, a: (0, i, 0, 0))
    result = pl.pallas_call(
        functools.partial(feed_kernel, subs=subs, size=size, first=first, last=last),
        out_shape=(
            jax.ShapeDtypeStruct((tokens, width), kind),
            jax.ShapeDtypeStruct((tokens, width), kind),
        )
        + (jax.ShapeDtypeStruct((places, subs, rows, cols), jnp.bfloat16),) * 4,
        grid_spec=pltpu.PrefetchScalarGridSpec(
            num_scalar_prefetch=1,
            grid=(subs,),
            in_specs=[whole, turned, whole, turned]
            + ([] if first else [whole, whole])
            + [ANYWHERE] * len(pieces),
            out_specs=(whole, whole) + (piece_spec,) * 4,
            scratch_shapes=[
                pltpu.VMEM((subs, width, cols), jnp.bfloat16),
                pltpu.VMEM((tokens, size), jnp.bfloat16),
                pltpu.VMEM((tokens, size), jnp.bfloat16),
                pltpu.VMEM((tokens, size), jnp.bfloat16),
                pltpu.VMEM((width, cols), jnp.float32),
                pltpu.VMEM((tokens, width), jnp.float32),
                pltpu.VMEM((tokens, width), jnp.float32),
                pltpu.SemaphoreType.DMA((subs, blocks)),
            ],
        ),
        compiler_params=params(),
        cost_estimate=cost(
            18 * tokens * width * size * subs,
            tokens * width * (8 + 16) + 4 * width * cols * subs,
        ),
    )(load_at, hidden, hidden_t, grad, grad_t, *(sums or ()), *pieces)
    return result[:2], list(result[2:])


def outer_kernel(load_at, grad, grad_t, mixed, *rest):
    pieces, mixed_grad, outs, (weights, total, sems) = rest[:-8], rest[-8], rest[-7:-3], rest[-3:]
    step = pl.program_id(0)
    block = mixed.shape[1]

    @pl.when(step == 0)
    def _():
        for copy in block_copies(pieces, weights, load_at, sems, None):
            copy.start()

    def weight_rows(index, rows):
        total[rows, :] = dense(grad_t[rows, :], mixed[...])

    each_head(grad_t.shape[0] // 512, 512, weight_rows)
    store_blocks(total, outs, load_at, True)

    @pl.when(step == 0)
    def _():
        for copy in block_copies(pieces, weights, load_at, sems, None):
            copy.wait()

    column = pl.ds(pl.multiple_of(step * block, block), block)

    def back_rows(rows):
        mixed_grad[rows, :] = dense(grad[rows, :], weights[:, column]).astype(jnp.bfloat16)

    each_rows(grad.shape[0], back_rows)


def outer_call(load_at, grad, grad_t, mixed, pieces, block, more):
    tokens, width = grad.shape
    cols = mixed.shape[1]
    places, rows, _ = pieces[0].shape
    subs = cols // block
    piece_spec = pl.BlockSpec((places, 1, rows, block), lambda i, a: (0, i, 0, 0))
    by_step = pl.BlockSpec((tokens, block), lambda i, a: (0, i))
    result = pl.pallas_call(
        outer_kernel,
        out_shape=(jax.ShapeDtypeStruct((tokens, cols), jnp.bfloat16),)
        + (jax.ShapeDtypeStruct((places, subs + more, rows, block), jnp.bfloat16),) * 4,
        grid_spec=pltpu.PrefetchScalarGridSpec(
            num_scalar_prefetch=1,
            grid=(subs,),
            in_specs=[fixed_two((tokens, width)), fixed_two((width, tokens)), by_step]
            + [ANYWHERE] * len(pieces),
            out_specs=(by_step,) + (piece_spec,) * 4,
            scratch_shapes=[
                pltpu.VMEM((width, cols), jnp.bfloat16),
                pltpu.VMEM((width, block), jnp.float32),
                pltpu.SemaphoreType.DMA((lax.axis_size(DP),)),
            ],
        ),
        compiler_params=params(),
        cost_estimate=cost(4 * tokens * width * cols, 4 * tokens * (width + cols) + 4 * width * cols),
    )(load_at, grad, grad_t, mixed, *pieces)
    return result[0], list(result[1:])


def back_kernel(
    load_at,
    hidden_t,
    cos_ref,
    sin_ref,
    gains,
    turned,
    raw,
    mixed,
    mixed_grad,
    lse_ref,
    *rest,
    kv_first,
    kv_count,
    sizes,
    per_group,
    group,
    head,
    eps,
    first,
    last,
):
    rest = list(rest)
    if first:
        sum_in = None
    else:
        sum_in = rest[0]
        rest = rest[1:]
    pieces = split_groups(rest, sizes)
    hidden_out, head_sum = rest[-14:-12]
    outs = rest[-12:-8]
    weights, d_query, d_key, d_value, d_all, total, hidden_sum, sems = rest[-8:]
    step = pl.program_id(0)
    tokens = raw.shape[0]
    width = hidden_t.shape[0]
    q_cols = group * head
    factor = head ** (-0.5)

    @pl.when(step == 0)
    def _():
        for lead in range(kv_count):
            for copy in head_copies(pieces, per_group, weights, load_at, sems, kv_first, lead):
                copy.start()
        head_sum[...] = jnp.zeros_like(head_sum)
        hidden_sum[...] = jnp.zeros_like(hidden_sum) if first else sum_in[...]

    d_key[...] = jnp.zeros_like(d_key)
    d_value[...] = jnp.zeros_like(d_value)

    def back_head(j, cols):
        for start, end in spans(tokens, 256):
            query = turned[start:end, cols]
            grad = mixed_grad[start:end, cols]
            delta = to_row(
                jnp.sum(
                    grad.astype(jnp.float32) * mixed[start:end, cols].astype(jnp.float32),
                    -1,
                    keepdims=True,
                )
            )
            shift = lse_ref[0, j, 0:1, start:end] * LOG2E
            grad_query = None
            for low, high in ((0, start), (start, end)):
                if low == high:
                    continue
                keys = turned[low:high, q_cols : q_cols + head]
                values = turned[low:high, q_cols + head :]
                scores = contract_cols(keys, query)
                probs = jnp.exp2(scores * (factor * LOG2E) - shift)
                if low == start:
                    probs = jnp.where(causal_t(0, high - low, 0, end - start), probs, 0.0)
                grad_probs = contract_cols(values, grad)
                grad_scores = (probs * (grad_probs - delta) * factor).astype(jnp.bfloat16)
                d_value[low:high, :] += dense(probs.astype(jnp.bfloat16), grad)
                d_key[low:high, :] += dense(grad_scores, query)
                term = contract_rows(grad_scores, keys)
                grad_query = term if grad_query is None else grad_query + term
            d_query[start:end, cols] = grad_query

    each_head(group, head, back_head)
    sums = [None, None]
    for j in range(group + 1):
        cols = slice(j * head, (j + 1) * head)
        which = 0 if j < group else 1
        for start, end in spans(tokens, 416):
            part = raw[start:end, cols]
            scale = lax.rsqrt(jnp.mean(part * part, -1, keepdims=True) + eps)
            normed = part * scale
            grad = d_query[start:end, cols] if j < group else d_key[start:end, :]
            grad = rotate_rows(grad, cos_ref[start:end, :], sin_ref[start:end, :], -1.0)
            product = jnp.sum(grad * normed, 0, keepdims=True)
            sums[which] = product if sums[which] is None else sums[which] + product
            grad = grad * gains[which : which + 1, :]
            d_all[start:end, cols] = (
                scale * (grad - normed * jnp.mean(grad * normed, -1, keepdims=True))
            ).astype(jnp.bfloat16)
    head_sum[0:1, :] += sums[0]
    head_sum[1:2, :] += sums[1]
    d_all[:, q_cols + head :] = d_value[...].astype(jnp.bfloat16)

    def weight_rows(index, rows):
        total[rows, :] = dense(hidden_t[rows, :], d_all[...])

    each_head(width // 512, 512, weight_rows)
    store_blocks(total, outs, load_at, True)
    for lead in range(kv_count):

        @pl.when(step == lead)
        def _():
            for copy in head_copies(pieces, per_group, weights, load_at, sems, kv_first, lead):
                copy.wait()

    def hidden_rows(rows):
        hidden_sum[rows, :] += contract_cols(d_all[rows, :], weights[step])

    each_rows(tokens, hidden_rows)

    @pl.when(step == kv_count - 1)
    def _():
        hidden_out[...] = hidden_sum[...].astype(hidden_out.dtype)


def head_copies(groups, per_group, buffer, offsets, sems, kv_first, lead):
    pieces = groups[(kv_first + lead) // per_group]
    inside = (kv_first + lead) % per_group
    rows = pieces[0].shape[-2]
    copies = []
    index = 0
    for piece in pieces:
        for place in range(piece.shape[0]):
            start = pl.multiple_of(offsets[index] * rows, rows)
            copies.append(
                pltpu.make_async_copy(
                    piece.at[place, inside],
                    buffer.at[lead, pl.ds(start, rows), :],
                    sems.at[lead, index],
                )
            )
            index += 1
    return copies


def split_groups(refs, sizes):
    groups = []
    for size in sizes:
        groups.append(refs[:size])
        refs = refs[size:]
    return groups


def back_call(
    load_at,
    hidden_t,
    tables,
    kept,
    mixed_grad,
    sum_in,
    groups,
    kv_first,
    kv_count,
    group,
    head,
    last,
    into,
):
    cos_two, sin_two, gains_t = tables
    turned, raw, mixed, lse_t = kept
    width, tokens = hidden_t.shape
    cols = (group + 2) * head
    raw_cols = (group + 1) * head
    pieces = [piece for one in groups for piece in one]
    places, per_group, rows, _ = pieces[0].shape
    blocks = lax.axis_size(DP)
    first = sum_in is None
    by_step = lambda i, a: (0, kv_first + i)
    into = list(into or ())
    subs = into[0].shape[1] if into else kv_count
    shift = subs - kv_count
    ahead = 10 + (0 if first else 1) + len(pieces)
    whole = fixed_two((tokens, width))
    result = pl.pallas_call(
        functools.partial(
            back_kernel,
            kv_first=kv_first,
            kv_count=kv_count,
            sizes=tuple(len(one) for one in groups),
            per_group=per_group,
            group=group,
            head=head,
            eps=norm_eps,
            first=first,
            last=last,
        ),
        out_shape=(
            jax.ShapeDtypeStruct((tokens, width), jnp.bfloat16 if last else jnp.float32),
            jax.ShapeDtypeStruct((8, head), jnp.float32),
        )
        + (jax.ShapeDtypeStruct((places, subs, rows, cols), jnp.bfloat16),) * 4,
        grid_spec=pltpu.PrefetchScalarGridSpec(
            num_scalar_prefetch=1,
            grid=(kv_count,),
            in_specs=[
                fixed_two((width, tokens)),
                fixed_two((tokens, head)),
                fixed_two((tokens, head)),
                fixed_two((2, head)),
                pl.BlockSpec((tokens, cols), by_step),
                pl.BlockSpec((tokens, raw_cols), by_step),
                pl.BlockSpec((tokens, group * head), by_step),
                pl.BlockSpec((tokens, group * head), by_step),
                pl.BlockSpec((1, group, 8, tokens), lambda i, a: (kv_first + i, 0, 0, 0)),
            ]
            + ([] if first else [whole])
            + [ANYWHERE] * (len(pieces) + len(into)),
            out_specs=(whole, fixed_two((8, head)))
            + (pl.BlockSpec((places, 1, rows, cols), lambda i, a: (0, shift + i, 0, 0)),) * 4,
            scratch_shapes=[
                pltpu.VMEM((kv_count, width, cols), jnp.bfloat16),
                pltpu.VMEM((tokens, group * head), jnp.float32),
                pltpu.VMEM((tokens, head), jnp.float32),
                pltpu.VMEM((tokens, head), jnp.float32),
                pltpu.VMEM((tokens, cols), jnp.bfloat16),
                pltpu.VMEM((width, cols), jnp.float32),
                pltpu.VMEM((tokens, width), jnp.float32),
                pltpu.SemaphoreType.DMA((kv_count, blocks)),
            ],
        ),
        input_output_aliases={ahead + k: 2 + k for k in range(len(into))},
        compiler_params=params(),
        cost_estimate=cost(
            4 * tokens * width * cols * kv_count + 7 * tokens * tokens * head * group * kv_count,
            tokens * (width * 6 + kv_count * (cols * 2 + raw_cols * 4 + group * head * 4))
            + width * cols * kv_count * 4,
        ),
    )(
        load_at,
        hidden_t,
        cos_two,
        sin_two,
        gains_t,
        turned,
        raw,
        mixed,
        mixed_grad,
        lse_t,
        *(() if first else (sum_in,)),
        *pieces,
        *into,
    )
    return result[0], result[1], list(result[2:])


def adam(param, grad, first, second, rate, decay):
    new_first = 0.9 * first + 0.1 * grad
    new_second = 0.95 * second + 0.05 * grad * grad
    fix_first = 1.0 - 0.9**ADAM_STEP
    fix_second = 1.0 - 0.95**ADAM_STEP
    step_size = new_first / fix_first / (jnp.sqrt(new_second / fix_second) + 1e-08)
    return (param - rate * (step_size + decay * param), new_first, new_second)


def own_rows(full, count):
    return lax.dynamic_slice_in_dim(full, lax.axis_index(DP) * count, count, 0)


def local(
    block_in,
    grad_out,
    query_weight,
    keyvalue_matrix,
    output_weight,
    feedfwd_weight,
    norm_gains,
    head_gains,
    first_query,
    keyvalue_first_moment,
    first_output,
    first_feedfwd,
    first_norm,
    first_head,
    second_query,
    keyvalue_second_moment,
    second_output,
    second_feedfwd,
    second_norm,
    second_head,
):
    tokens = block_in.shape[0]
    width = block_in.shape[1]
    head_size = head_gains.shape[0]
    group = QUERY_HEADS // KEYVALUE_HEADS
    keyvalue_columns = keyvalue_matrix.shape[2]
    kv_local = keyvalue_columns // head_size
    ffn_local = feedfwd_weight.shape[2]
    q_cols = group * head_size
    half_type = jnp.bfloat16
    grad_scale = float(tokens * lax.axis_size(DP)) ** (-0.5)
    load_at = block_places()
    size = 256 if ffn_local % 512 == 0 else 128
    per_call = 2 if ffn_local % (2 * size) == 0 else 1
    if ffn_local // (per_call * size) > 3 or ffn_local % (per_call * size):
        per_call = ffn_local // size
    calls = ffn_local // (per_call * size)

    packed = jnp.stack(
        [
            jnp.concatenate(
                [
                    query_weight[:, n * q_cols : (n + 1) * q_cols],
                    keyvalue_matrix[:, 0, n * head_size : (n + 1) * head_size],
                    keyvalue_matrix[:, 1, n * head_size : (n + 1) * head_size],
                ],
                1,
            ).astype(half_type)
            for n in range(kv_local)
        ]
    )
    feed_parts = []
    for c in range(calls):
        blocks = []
        for b in range(c * per_call, (c + 1) * per_call):
            blocks.append(
                jnp.concatenate(
                    [feedfwd_weight[:, t, b * size : (b + 1) * size] for t in range(3)], 1
                ).astype(half_type)
            )
        feed_parts.append(jnp.stack(blocks))
    per_group = 2 if kv_local % 2 == 0 else kv_local
    qkv_pieces = [
        plane_gather(line_gather(packed[c * per_group : (c + 1) * per_group]), BOTH)
        for c in range(kv_local // per_group)
    ]
    out_pieces = plane_gather(line_gather(output_weight.astype(half_type)), BOTH)
    feed_pieces = [plane_gather(line_gather(part), BOTH) for part in feed_parts]

    gains_two = norm_gains.T
    tables = rot_table(tokens, head_size) + (head_gains.T,)
    full = jnp.float32
    hidden_one, hidden_one_t, grad_out_t = row_call(
        prepare_kernel,
        (block_in, grad_out, gains_two),
        (("r", half_type), ("t", half_type), ("t", half_type)),
        10,
    )
    kept = None
    for c in range(kv_local):
        kept = attend_call(
            load_at,
            hidden_one,
            *tables,
            qkv_pieces[c // per_group],
            c % per_group,
            c,
            kv_local,
            group,
            head_size,
            kept,
        )
    mixed = kept[2]
    attn_half = project_call(load_at, [mixed], out_pieces)
    resid, hidden_two, hidden_two_t = row_call(
        middle_kernel,
        (block_in, *tensor_terms(attn_half), gains_two),
        (("r", full), ("r", half_type), ("t", half_type)),
        14,
    )

    sums = None
    feed_rows = []
    for c in range(calls):
        sums, grads = feed_call(
            load_at,
            hidden_two,
            hidden_two_t,
            grad_out,
            grad_out_t,
            sums,
            feed_pieces[c],
            size,
            c == calls - 1,
        )
        feed_rows.append(plane_sum(grads, SECOND if c % 2 == 0 else FIRST))
    ffn_half, grad_hidden_half = sums
    grad_resid, grad_resid_half, grad_resid_half_t, gain_two = row_call(
        functools.partial(late_kernel, tokens=tokens),
        (resid, grad_out, *tensor_terms(grad_hidden_half), gains_two),
        (("r", full), ("r", half_type), ("t", half_type), ("s", full)),
        18,
    )
    left, right = tensor_terms(ffn_half)
    block_out = (resid + (left.astype(full) + right.astype(full))).astype(half_type)
    columns = (group + 2) * head_size
    block = columns if mixed.shape[1] % columns == 0 else mixed.shape[1]
    mixed_gradient, grads = outer_call(
        load_at,
        grad_resid_half,
        grad_resid_half_t,
        mixed,
        out_pieces,
        block,
        0,
    )
    output_blocks = plane_sum(grads, FIRST)
    hidden_part = None
    head_part = None
    packed_rows = []
    for start in range(0, kv_local, per_group):
        count = per_group
        hidden_part, heads, grads = back_call(
            load_at,
            hidden_one_t,
            tables,
            kept,
            mixed_gradient,
            hidden_part,
            qkv_pieces,
            start,
            count,
            group,
            head_size,
            start + count == kv_local,
            None,
        )
        head_part = heads if head_part is None else head_part + heads
        rows_sum = plane_sum(grads, SECOND)
        packed_rows.append(rows_sum)
    by_block = line_sum(feed_rows[:1])
    if calls > 1:
        by_block += line_sum(feed_rows[1:])
    (output_rows,) = line_sum([output_blocks])
    by_head = []
    for part in packed_rows:
        by_head += line_sum([part])
    output_rows = jnp.concatenate(list(output_rows), 1)
    grad_input, gain_one = row_call(
        functools.partial(final_kernel, tokens=tokens),
        (block_in, grad_resid, *tensor_terms(hidden_part), gains_two),
        (("r", half_type), ("s", full)),
        12,
    )
    left, right = tensor_terms(head_part[:2].astype(half_type))
    head_both = left.astype(full) + right.astype(full)
    small = jnp.concatenate(
        [gain_one[0].reshape(-1, 128), gain_two[0].reshape(-1, 128), head_both.reshape(-1, 128)]
    )
    small = all_sum_small(small)
    lanes = width // 128
    grad_norm = jnp.stack(
        [small[:lanes].reshape(width), small[lanes : 2 * lanes].reshape(width)], 1
    )
    grad_head = small[2 * lanes :].reshape(2, head_size).T
    norm_rows = own_rows(grad_norm, first_norm.shape[0]) * grad_scale
    head_rows = own_rows(grad_head, first_head.shape[0]) * grad_scale

    by_head = jnp.concatenate(by_head)
    query_rows = jnp.concatenate([by_head[n, :, :q_cols] for n in range(kv_local)], 1) * grad_scale
    keyvalue_rows = (
        jnp.stack(
            [
                jnp.concatenate(
                    [
                        by_head[n, :, q_cols + t * head_size : q_cols + (t + 1) * head_size]
                        for n in range(kv_local)
                    ],
                    1,
                )
                for t in range(2)
            ],
            1,
        )
        * grad_scale
    )
    output_rows = output_rows * grad_scale
    by_block = jnp.concatenate(by_block)
    feedfwd_grad_rows = (
        jnp.stack(
            [
                jnp.concatenate(
                    [
                        by_block[b, :, t * size : (t + 1) * size]
                        for b in range(ffn_local // size)
                    ],
                    1,
                )
                for t in range(3)
            ],
            1,
        )
        * grad_scale
    )
    norm_own = own_rows(norm_gains, first_norm.shape[0])
    head_own = own_rows(head_gains, first_head.shape[0])
    new_query, new_first_query, new_second_query = adam(
        query_weight, query_rows, first_query, second_query, 0.01, 0.1
    )
    new_keyvalue, new_first_keyvalue, new_second_keyvalue = adam(
        keyvalue_matrix, keyvalue_rows, keyvalue_first_moment, keyvalue_second_moment, 0.01, 0.1
    )
    new_output, new_first_output, new_second_output = adam(
        output_weight, output_rows, first_output, second_output, 0.01, 0.1
    )
    new_feedfwd, new_first_feedfwd, new_second_feedfwd = adam(
        feedfwd_weight, feedfwd_grad_rows, first_feedfwd, second_feedfwd, 0.01, 0.1
    )
    new_norm, new_first_norm, new_second_norm = adam(
        norm_own, norm_rows, first_norm, second_norm, 0.1, 0.0
    )
    new_head, new_first_head, new_second_head = adam(
        head_own, head_rows, first_head, second_head, 0.1, 0.0
    )
    return (
        block_out,
        grad_input,
        query_rows,
        keyvalue_rows,
        output_rows,
        feedfwd_grad_rows,
        norm_rows,
        head_rows,
        new_query,
        new_keyvalue,
        new_output,
        new_feedfwd,
        new_norm,
        new_head,
        new_first_query,
        new_first_keyvalue,
        new_first_output,
        new_first_feedfwd,
        new_first_norm,
        new_first_head,
        new_second_query,
        new_second_keyvalue,
        new_second_output,
        new_second_feedfwd,
        new_second_norm,
        new_second_head,
    )


def solution(mesh):
    placed = (
        ROWS,
        ROWS,
        FLAT,
        DEEP,
        FLAT,
        DEEP,
        P(),
        P(),
        FLAT,
        DEEP,
        FLAT,
        DEEP,
        ROWS,
        ROWS,
        FLAT,
        DEEP,
        FLAT,
        DEEP,
        ROWS,
        ROWS,
    )
    return jax.shard_map(
        local,
        mesh=mesh,
        in_specs=placed,
        out_specs=(
            ROWS,
            ROWS,
            FLAT,
            DEEP,
            FLAT,
            DEEP,
            ROWS,
            ROWS,
            FLAT,
            DEEP,
            FLAT,
            DEEP,
            ROWS,
            ROWS,
            FLAT,
            DEEP,
            FLAT,
            DEEP,
            ROWS,
            ROWS,
            FLAT,
            DEEP,
            FLAT,
            DEEP,
            ROWS,
            ROWS,
        ),
        check_vma=False,
    )
```
